32 devices in a mesh: ctx: 16 (over z, y, core), heads: 2 (over x).
Axes of the slice: x: 2, y: 2, z: 4, core: 2. Of those that a mesh axis runs over, the one named last changes fastest.
Arguments:
- activations: bfloat16 [5376, 16384], P('heads', 'ctx'), may hold values from -6 to 6
- frozen_query_rows: bfloat16 [16384, 4096], P('ctx', 'heads'), may hold values from -100 to 100
- frozen_key_rows: bfloat16 [16384, 2048], P('ctx', 'heads'), may hold values from -6 to 6
- frozen_value_rows: bfloat16 [16384, 2048], P('ctx', 'heads'), may hold values from -6 to 6
- output_gradient: bfloat16 [16384, 4096], P('ctx', 'heads'), may hold values from -0.5 to 0.5
- query_down_weight: bfloat16 [5376, 16], P('heads'), may hold values from -0.078125 to 0.078125
- query_up_weight: bfloat16 [16, 4096], P(None, 'heads'), may hold values from -0.0390625 to 0.0390625
- key_down_weight: bfloat16 [5376, 16], P('heads'), may hold values from -0.078125 to 0.078125
- key_up_weight: bfloat16 [16, 2048], P(None, 'heads'), may hold values from -0.0390625 to 0.0390625
- value_down_weight: bfloat16 [5376, 16], P('heads'), may hold values from -0.078125 to 0.078125
- value_up_weight: bfloat16 [16, 2048], P(None, 'heads'), may hold values from -0.0390625 to 0.0390625
Outputs:
- query_down_gradient: float32 [5376, 16], P('heads')
- query_up_gradient: float32 [16, 4096], P(None, 'heads')
- key_down_gradient: float32 [5376, 16], P('heads')
- key_up_gradient: float32 [16, 2048], P(None, 'heads')
- value_down_gradient: float32 [5376, 16], P('heads')
- value_up_gradient: float32 [16, 2048], P(None, 'heads')
The draws below stay inside these ranges and needn't reach their ends.
All inputs are finite; a program needn't handle non-finite values.
Results may differ from the reference program's by a relative error of at most 0.0098.
Values may be sent and summed in bfloat16 or wider, within the bound.
No kernel may reach another device: no remote copies, remote signals or barrier semaphores. Data moves between devices by JAX's collectives and lax.ppermute only.
A program may use at most 256 MiB of HBM per device.

```python
import jax
import jax.numpy as jnp
from jax import lax

MODEL_WIDTH = 5376
QUERY_HEAD_COUNT = 32
KEY_VALUE_HEADS = 16
HEAD_WIDTH = 128
WINDOW = 1024
ADAPTER_RANK = 16
TOK_DEV = 1024
TOKEN_COUNT = 16384


def drawn_pair(key):
    folded = jax.random.fold_in(key, 4242)
    seed_query, initial_key_rows = jax.random.split(folded, 2)
    sequence_length = TOKEN_COUNT
    key_rows = jnp.clip(jax.random.normal(initial_key_rows, (sequence_length, KEY_VALUE_HEADS * HEAD_WIDTH), jnp.float32), -6.0, 6.0)
    query_matrix = jnp.clip(jax.random.normal(seed_query, (sequence_length, QUERY_HEAD_COUNT * HEAD_WIDTH), jnp.float32), -6.0, 6.0)
    return (query_matrix, key_rows)


def draw_frozen_query_rows(key, part):
    return drawn_pair(key)[0].astype(jnp.bfloat16)


def draw_frozen_key_rows(key, part):
    return drawn_pair(key)[1].astype(jnp.bfloat16)


def steps_of(stream_key, extent, shards, least, largest):
    factor_of = 1.0
    for dim, blocks in shards:
        steps = jax.random.uniform(jax.random.fold_in(jax.random.fold_in(stream_key, 6), dim), (blocks,), jnp.float32, least / len(shards), largest / len(shards))
        factor_of = factor_of * jnp.repeat(jnp.exp(steps), extent[dim] // blocks).reshape((-1,) + (1,) * (len(extent) - 1 - dim))
    return factor_of


def normal_values(key, shape, width, limit, shards=(), kind=jnp.bfloat16):
    array = width * jax.random.normal(key, shape, jnp.float32)
    if shards:
        array = array * steps_of(key, shape, shards, -0.22, 0.18)
    return jnp.clip(array, -limit, limit).astype(kind)


def setup_inputs(seed: int = 0) -> dict:
    key_list = jax.random.split(jax.random.key(seed), 12)
    return {
        "activations": normal_values(key_list[0], (MODEL_WIDTH, TOKEN_COUNT), 1.0, 6.0, ((0, 2), (1, 16))),
        "frozen_query_rows": draw_frozen_query_rows(jax.random.fold_in(key_list[11], 71), 0),
        "frozen_key_rows": draw_frozen_key_rows(jax.random.fold_in(key_list[11], 71), 0),
        "frozen_value_rows": normal_values(key_list[3], (TOKEN_COUNT, KEY_VALUE_HEADS * HEAD_WIDTH), 1.0, 6.0, ((0, 16), (1, 2))),
        "output_gradient": normal_values(key_list[4], (TOKEN_COUNT, QUERY_HEAD_COUNT * HEAD_WIDTH), 0.08, 0.5, ((0, 16), (1, 2))),
        "query_down_weight": normal_values(key_list[5], (MODEL_WIDTH, ADAPTER_RANK), MODEL_WIDTH ** -0.5, 0.078125, ((0, 2),)),
        "query_up_weight": normal_values(key_list[6], (ADAPTER_RANK, QUERY_HEAD_COUNT * HEAD_WIDTH), (ADAPTER_RANK * 1600) ** -0.5, 0.0390625, ((1, 2),)),
        "key_down_weight": normal_values(key_list[7], (MODEL_WIDTH, ADAPTER_RANK), MODEL_WIDTH ** -0.5, 0.078125, ((0, 2),)),
        "key_up_weight": normal_values(key_list[8], (ADAPTER_RANK, KEY_VALUE_HEADS * HEAD_WIDTH), (ADAPTER_RANK * 1600) ** -0.5, 0.0390625, ((1, 2),)),
        "value_down_weight": normal_values(key_list[9], (MODEL_WIDTH, ADAPTER_RANK), MODEL_WIDTH ** -0.5, 0.078125, ((0, 2),)),
        "value_up_weight": normal_values(key_list[10], (ADAPTER_RANK, KEY_VALUE_HEADS * HEAD_WIDTH), (ADAPTER_RANK * 1600) ** -0.5, 0.0390625, ((1, 2),)),
    }


adapter_scale = 2.0
highest_precision = lax.Precision.HIGHEST

def band_grad(query_matrix, key_rows, value_rows, output_gradient, offset, leading):
    rows_here = query_matrix.shape[0]
    span = key_rows.shape[0]
    window = span - rows_here
    head_size = HEAD_WIDTH
    kv_heads = key_rows.shape[1] // head_size
    query_group_width = query_matrix.shape[1] // (kv_heads * head_size)
    scale = head_size ** (-0.5)
    query_heads = query_matrix.astype(jnp.float32).reshape(rows_here, kv_heads, query_group_width, head_size)
    key_heads = key_rows.astype(jnp.float32).reshape(span, kv_heads, head_size)
    value_heads = value_rows.astype(jnp.float32).reshape(span, kv_heads, head_size)
    grad_heads = output_gradient.astype(jnp.float32).reshape(rows_here, kv_heads, query_group_width, head_size)
    scores = scale * jnp.einsum('qhgd,khd->hgqk', query_heads, key_heads)
    query_pos = jnp.arange(rows_here, dtype=jnp.int32)[:, None]
    key_pos = jnp.arange(span, dtype=jnp.int32)[None, :]
    allowed = (key_pos > query_pos) & (key_pos <= query_pos + window)
    allowed = allowed & ((key_pos + offset >= window) | jnp.logical_not(leading))
    scores = jnp.where(allowed, scores, -jnp.inf)
    highest_score = lax.optimization_barrier(jnp.max(scores, axis=-1, keepdims=True))
    exponent = jnp.exp(scores - highest_score)
    weights = exponent / lax.optimization_barrier(jnp.sum(exponent, axis=-1, keepdims=True))
    weights_low = lax.optimization_barrier(weights.astype(jnp.bfloat16)).astype(jnp.float32)
    attended = jnp.einsum('hgqk,khd->qhgd', weights_low, value_heads)
    row_dots = jnp.einsum('qhgd,qhgd->hgq', grad_heads, attended)
    grad_weights = jnp.einsum('qhgd,khd->hgqk', grad_heads, value_heads)
    grad_scores = scale * weights * (grad_weights - row_dots[..., None])
    grad_low = lax.optimization_barrier(grad_scores.astype(jnp.bfloat16)).astype(jnp.float32)
    query_gradient_rows = jnp.einsum('hgqk,khd->qhgd', grad_low, key_heads).reshape(rows_here, -1)
    key_gradient_rows = jnp.einsum('hgqk,qhgd->khd', grad_low, query_heads).reshape(span, -1)
    value_gradient_rows = jnp.einsum('hgqk,qhgd->khd', weights_low, grad_heads).reshape(span, -1)
    return (query_gradient_rows, key_gradient_rows, value_gradient_rows)

def adapted_output(base_output, rank_portion, adapter_up_weight):
    lifted_rows = jnp.dot(rank_portion, adapter_up_weight.astype(jnp.float32), precision=highest_precision)
    return (base_output.astype(jnp.float32) + adapter_scale * lifted_rows).astype(jnp.bfloat16)

def reference(activations, frozen_query_rows, frozen_key_rows, frozen_value_rows, output_gradient, query_down_weight, query_up_weight, key_down_weight, key_up_weight, value_down_weight, value_up_weight):
    query_rank_rows = jnp.dot(activations.T, query_down_weight, preferred_element_type=jnp.float32)
    key_rank_rows = jnp.dot(activations.T, key_down_weight, preferred_element_type=jnp.float32)
    value_rank_rows = jnp.dot(activations.T, value_down_weight, preferred_element_type=jnp.float32)
    query_matrix = adapted_output(frozen_query_rows, query_rank_rows, query_up_weight)
    key_rows = adapted_output(frozen_key_rows, key_rank_rows, key_up_weight)
    value_rows = adapted_output(frozen_value_rows, value_rank_rows, value_up_weight)
    width_k = key_rows.shape[1]
    padding = jnp.zeros((WINDOW, width_k), jnp.bfloat16)
    keys_long = jnp.concatenate([padding, key_rows], axis=0)
    values_long = jnp.concatenate([padding, value_rows], axis=0)
    block_count = TOKEN_COUNT // TOK_DEV

    def one_block(block_index):
        start = block_index * TOK_DEV
        query_rows = lax.dynamic_slice_in_dim(query_matrix, start, TOK_DEV, 0)
        grad_rows = lax.dynamic_slice_in_dim(output_gradient, start, TOK_DEV, 0)
        key_span = lax.dynamic_slice_in_dim(keys_long, start, TOK_DEV + WINDOW, 0)
        value_span = lax.dynamic_slice_in_dim(values_long, start, TOK_DEV + WINDOW, 0)
        return band_grad(query_rows, key_span, value_span, grad_rows, jnp.int32(0), block_index == 0)
    query_gradient_rows, key_spans, value_spans = lax.map(one_block, jnp.arange(block_count, dtype=jnp.int32))
    query_gradient_rows = query_gradient_rows.reshape(TOKEN_COUNT, -1)

    def settle(spans):
        own = spans[:, WINDOW:]
        earlier = jnp.concatenate([spans[1:, :WINDOW], jnp.zeros((1, WINDOW, width_k), spans.dtype)], axis=0)
        earlier = jnp.concatenate([jnp.zeros((block_count, TOK_DEV - WINDOW, width_k), spans.dtype), earlier], axis=1)
        return (own + earlier).reshape(TOKEN_COUNT, width_k)
    key_gradient_rows = settle(key_spans)
    value_gradient_rows = settle(value_spans)
    widened_input_rows = activations.astype(jnp.float32)

    def adapter_branch(gradient_rows, rank_portion, adapter_up_weight):
        inner_function = jnp.dot(gradient_rows, adapter_up_weight.astype(jnp.float32).T, precision=highest_precision)
        down_gradient = adapter_scale * jnp.dot(widened_input_rows, inner_function, precision=highest_precision)
        up_gradient = adapter_scale * jnp.dot(rank_portion.T, gradient_rows, precision=highest_precision)
        return (down_gradient, up_gradient)
    query_down_gradient, query_up_gradient = adapter_branch(query_gradient_rows, query_rank_rows, query_up_weight)
    key_down_gradient, key_up_gradient = adapter_branch(key_gradient_rows, key_rank_rows, key_up_weight)
    value_down_gradient, value_up_gradient = adapter_branch(value_gradient_rows, value_rank_rows, value_up_weight)
    return (query_down_gradient, query_up_gradient, key_down_gradient, key_up_gradient, value_down_gradient, value_up_gradient)
```

```python
import functools

import jax
import jax.numpy as jnp
from jax import lax
from jax.experimental import pallas as pl
from jax.experimental.pallas import tpu as pltpu
from jax.sharding import PartitionSpec as P

HEAD_WIDTH = 128
WINDOW = 1024
ADAPTER_SCALE = 2.0
NEGATIVE = -1e30
LOG2E = 1.4426950408889634
F32 = jnp.float32
BF16 = jnp.bfloat16


def split2(x):
    high = x.astype(BF16)
    return high, (x - high.astype(F32)).astype(BF16)


def split3(x):
    high = x.astype(BF16)
    rest = x - high.astype(F32)
    middle = rest.astype(BF16)
    return high, middle, (rest - middle.astype(F32)).astype(BF16)


def dot_nn(a, b):
    return lax.dot_general(a, b, (((1,), (0,)), ((), ())), preferred_element_type=F32)


def dot_nt(a, b):
    return lax.dot_general(a, b, (((1,), (1,)), ((), ())), preferred_element_type=F32)


def fold8(x, reduce):
    return reduce(x.reshape(x.shape[0] // 8, 8, x.shape[1]), axis=0)


def attention_body(
    group,
    rank,
    bias_ref,
    rank_ref,
    prior_rank_ref,
    fq_ref,
    do_ref,
    fk_ref,
    pk_ref,
    fv_ref,
    pv_ref,
    uq_ref,
    uk_ref,
    uv_ref,
    inner_ref,
    inner_prior_ref,
    upq_ref,
    upk_ref,
    upv_ref,
    ranks_t,
    ranks,
    k_all,
    v_all,
    k_t,
    dk_acc,
    dv_acc,
    s_scr,
    dp_scr,
):
    head = pl.program_id(0)
    block = pl.program_id(1)
    rows = fq_ref.shape[0]
    own = fk_ref.shape[0]
    width = HEAD_WIDTH
    tiles = own // rows
    scale = width**-0.5
    factor = scale * LOG2E

    @pl.when((head == 0) & (block == 0))
    def _():
        mine = split3(rank_ref[...])
        prior = split3(prior_rank_ref[...])
        blank = jnp.zeros((rank, own), BF16)
        for part in range(3):
            at = part * 3 * rank
            ranks_t[at : at + 3 * rank, own:] = mine[part]
            ranks_t[at : at + rank, :own] = blank
            ranks_t[at + rank : at + 3 * rank, :own] = prior[part]
        ranks[...] = ranks_t[...].astype(F32).T.astype(BF16)
        inner_ref[...] = jnp.zeros_like(inner_ref)
        inner_prior_ref[...] = jnp.zeros_like(inner_prior_ref)

    def stacked(up, kind):
        pieces = []
        for _ in range(3):
            for other in range(3):
                pieces.append(up if other == kind else jnp.zeros_like(up))
        return jnp.concatenate(pieces, axis=0)

    def rank_rows(kind, start, size):
        pieces = [
            ranks_t[(3 * part + kind) * rank : (3 * part + kind + 1) * rank, pl.ds(start, size)]
            for part in range(3)
        ]
        return jnp.concatenate(pieces, axis=0)

    def merged(x):
        return x[:rank] + x[rank : 2 * rank] + x[2 * rank :]

    def lifted(base, rank_part, up):
        return (base.astype(F32) + ADAPTER_SCALE * dot_nn(rank_part, up)).astype(BF16)

    @pl.when(block == 0)
    def _():
        up_k = stacked(uk_ref[...], 1)
        up_v = stacked(uv_ref[...], 2)
        k_all[:own] = lifted(pk_ref[...], ranks[:own], up_k)
        k_all[own:] = lifted(fk_ref[...], ranks[own:], up_k)
        v_all[:own] = lifted(pv_ref[...], ranks[:own], up_v)
        v_all[own:] = lifted(fv_ref[...], ranks[own:], up_v)
        k_t[...] = k_all[...].T
        dk_acc[...] = jnp.zeros_like(dk_acc)
        dv_acc[...] = jnp.zeros_like(dv_acc)
        upq_ref[...] = jnp.zeros_like(upq_ref)

    base = pl.multiple_of(block * rows, rows)

    def at(tile):
        return pl.multiple_of(base + tile * rows, rows)

    rank_part = ranks[pl.ds(at(tiles), rows), :]
    q = lifted(fq_ref[...], rank_part, stacked(uq_ref[...], 0))
    q_cat = jnp.concatenate([q[:, g * width : (g + 1) * width] for g in range(group)], axis=0)
    do = do_ref[...]
    do_t = jnp.concatenate([do[:, g * width : (g + 1) * width].T for g in range(group)], axis=1)
    key_at = lax.broadcasted_iota(jnp.int32, (rows, rows), 0)
    query_at = lax.broadcasted_iota(jnp.int32, (rows, rows), 1)
    earlier = jnp.concatenate([key_at > query_at] * group, axis=1)
    bias = bias_ref[0]

    biases = []
    highest = None
    for tile in range(tiles):
        tile_bias = jnp.where(block + tile < tiles, bias, 0.0)
        scores = dot_nt(k_all[pl.ds(at(tile), rows), :], q_cat)
        grads = dot_nn(v_all[pl.ds(at(tile), rows), :], do_t)
        if tile == 0:
            last = dot_nt(k_all[pl.ds(at(tiles), rows), :], q_cat)
            scores = jnp.where(earlier, scores + bias, last)
            grads = jnp.where(earlier, grads, dot_nn(v_all[pl.ds(at(tiles), rows), :], do_t))
            tile_bias = jnp.float32(0.0)
        biases.append(tile_bias)
        s_scr[tile] = scores
        dp_scr[tile] = grads
        high = fold8(scores, jnp.max) + tile_bias
        highest = high if highest is None else jnp.maximum(highest, high)
    top = jnp.max(highest, axis=0, keepdims=True) * factor
    total = jnp.zeros((8, group * rows), F32)
    dots = jnp.zeros((8, group * rows), F32)
    for tile in range(tiles):
        exponent = jnp.exp2(s_scr[tile] * factor - (top - biases[tile]))
        s_scr[tile] = exponent
        total = total + fold8(exponent, jnp.sum)
        dots = dots + fold8(exponent * dp_scr[tile], jnp.sum)
    inverse = 1.0 / jnp.sum(total, axis=0, keepdims=True)
    row_dots = jnp.sum(dots, axis=0, keepdims=True) * inverse
    do_scaled = (do_t.astype(F32) * inverse).astype(BF16)
    column = jnp.broadcast_to(inverse, (8, group * rows)).T[:, :1]
    q_scaled = (q_cat.astype(F32) * column).astype(BF16)
    dq_t = jnp.zeros((width, group * rows), F32)

    def spread(tile, grad_low, weight_low):
        dk_acc[pl.ds(at(tile), rows), :] += dot_nn(grad_low, q_scaled)
        dv_acc[pl.ds(at(tile), rows), :] += dot_nt(weight_low, do_scaled)
        return dot_nn(k_t[:, pl.ds(at(tile), rows)], grad_low)

    for tile in range(tiles):
        exponent = s_scr[tile]
        grad = exponent * (dp_scr[tile] - row_dots)
        if tile == 0:
            zero = jnp.zeros_like(grad)
            dq_t = dq_t + spread(
                0,
                jnp.where(earlier, grad, zero).astype(BF16),
                jnp.where(earlier, exponent, zero).astype(BF16),
            )
            dq_t = dq_t + spread(
                tiles,
                jnp.where(earlier, zero, grad).astype(BF16),
                jnp.where(earlier, zero, exponent).astype(BF16),
            )
        else:
            dq_t = dq_t + spread(tile, grad.astype(BF16), exponent.astype(BF16))

    dq = dq_t * (inverse * scale)
    up_q = uq_ref[...]
    rank_q = rank_rows(0, at(tiles), rows)
    for part in split2(dq):
        tall = jnp.concatenate([part[:, g * rows : (g + 1) * rows] for g in range(group)], axis=0)
        inner_ref[:rank, pl.ds(base, rows)] += dot_nn(up_q, tall)
        upq_ref[...] += merged(dot_nt(rank_q, tall))

    @pl.when(block == tiles - 1)
    def _():
        for kind, acc, up_ref, out_ref, mult in (
            (1, dk_acc, uk_ref, upk_ref, scale),
            (2, dv_acc, uv_ref, upv_ref, 1.0),
        ):
            rank_part = rank_rows(kind, 0, 2 * own)
            high, low = split2(acc[...] * mult)
            out_ref[...] = merged(dot_nn(rank_part, high) + dot_nn(rank_part, low))
            inner = dot_nt(up_ref[...], high) + dot_nt(up_ref[...], low)
            inner_prior_ref[(kind - 1) * rank : kind * rank, :] += inner[:, :own]
            inner_ref[kind * rank : (kind + 1) * rank, :] += inner[:, own:]


def attention(first, heads, bias, rank_t, prior_rank_t, fq, do, fk, pk, fv, pv, uq, uk, uv, rows=256):
    rank = uq.shape[0]
    own = fk.shape[0]
    width = HEAD_WIDTH
    group = fq.shape[1] // fk.shape[1]
    wide = group * width
    tiles = own // rows
    whole = lambda h, b: (0, 0)
    query = lambda h, b: (b, first + h)
    key = lambda h, b: (0, first + h)
    chunk = lambda h, b: (0, h)
    in_specs = [
        pl.BlockSpec(memory_space=pltpu.SMEM),
        pl.BlockSpec(rank_t.shape, whole),
        pl.BlockSpec(prior_rank_t.shape, whole),
        pl.BlockSpec((rows, wide), query),
        pl.BlockSpec((rows, wide), query),
        pl.BlockSpec((own, width), key),
        pl.BlockSpec((own, width), chunk),
        pl.BlockSpec((own, width), key),
        pl.BlockSpec((own, width), chunk),
        pl.BlockSpec((rank, wide), key),
        pl.BlockSpec((rank, width), key),
        pl.BlockSpec((rank, width), key),
    ]
    out_specs = [
        pl.BlockSpec((3 * rank, own), whole),
        pl.BlockSpec((2 * rank, own), whole),
        pl.BlockSpec((rank, wide), chunk),
        pl.BlockSpec((rank, width), chunk),
        pl.BlockSpec((rank, width), chunk),
    ]
    out_shape = [
        jax.ShapeDtypeStruct((3 * rank, own), F32),
        jax.ShapeDtypeStruct((2 * rank, own), F32),
        jax.ShapeDtypeStruct((rank, heads * wide), F32),
        jax.ShapeDtypeStruct((rank, heads * width), F32),
        jax.ShapeDtypeStruct((rank, heads * width), F32),
    ]
    scratch = [
        pltpu.VMEM((9 * rank, 2 * own), BF16),
        pltpu.VMEM((2 * own, 9 * rank), BF16),
        pltpu.VMEM((2 * own, width), BF16),
        pltpu.VMEM((2 * own, width), BF16),
        pltpu.VMEM((width, 2 * own), BF16),
        pltpu.VMEM((2 * own, width), F32),
        pltpu.VMEM((2 * own, width), F32),
        pltpu.VMEM((tiles, rows, group * rows), F32),
        pltpu.VMEM((tiles, rows, group * rows), F32),
    ]
    pairs = heads * group * own * own
    return pl.pallas_call(
        functools.partial(attention_body, group, rank),
        grid=(heads, tiles),
        in_specs=in_specs,
        out_specs=out_specs,
        out_shape=out_shape,
        scratch_shapes=scratch,
        compiler_params=pltpu.CompilerParams(
            dimension_semantics=("arbitrary", "arbitrary"), vmem_limit_bytes=48 * 2**20
        ),
        cost_estimate=pl.CostEstimate(
            flops=10 * pairs * width,
            transcendentals=pairs,
            bytes_accessed=heads * own * width * (4 * group + 8),
        ),
        name="banded_attention",
    )(bias, rank_t, prior_rank_t, fq, do, fk, pk, fv, pv, uq, uk, uv)


def shifted(shard, axis, by):
    length = lax.axis_size(axis)
    pairs = [(i, i + by) for i in range(length) if 0 <= i + by < length]
    return lax.ppermute(shard, axis, pairs)


def summed(shard, axis):
    length = lax.axis_size(axis)
    if length & (length - 1):
        return lax.psum(shard, axis)
    step = 1
    while step < length:
        pairs = [(i, i ^ step) for i in range(length)]
        shard = shard + lax.ppermute(shard, axis, pairs)
        step *= 2
    return shard


def reduced(shard, axis):
    length = lax.axis_size(axis)
    if length & (length - 1):
        return lax.psum(shard, axis)
    index = lax.axis_index(axis)
    step = 1
    while step < length:
        pairs = [(i, i ^ step) for i in range(length)]
        half = shard.shape[1] // 2
        first, second = shard[:, :half], shard[:, half:]
        low = (index // step) % 2 == 0
        kept = jnp.where(low, first, second)
        sent = jnp.where(low, second, first)
        shard = kept + lax.ppermute(sent, axis, pairs)
        step *= 2
    while step > 1:
        step //= 2
        pairs = [(i, i ^ step) for i in range(length)]
        low = (index // step) % 2 == 0
        other = lax.ppermute(shard, axis, pairs)
        first, second = jnp.where(low, shard, other), jnp.where(low, other, shard)
        shard = jnp.concatenate([first, second], axis=1)
    return shard


def on_device(
    activations,
    frozen_query_rows,
    frozen_key_rows,
    frozen_value_rows,
    output_gradient,
    query_down_weight,
    query_up_weight,
    key_down_weight,
    key_up_weight,
    value_down_weight,
    value_up_weight,
):
    rank = query_down_weight.shape[1]
    features = activations.shape[0]
    heads = frozen_key_rows.shape[1] // HEAD_WIDTH
    per_call = max(1, heads // 4)
    prior = []
    for first in range(0, heads, per_call):
        columns = slice(first * HEAD_WIDTH, (first + per_call) * HEAD_WIDTH)
        prior.append(
            shifted((frozen_key_rows[:, columns], frozen_value_rows[:, columns]), "ctx", 1)
        )
    down = jnp.concatenate([query_down_weight, key_down_weight, value_down_weight], axis=1)
    partial_rank = lax.dot_general(
        down, activations, (((0,), (0,)), ((), ())), preferred_element_type=F32
    )
    rank_t = summed(partial_rank, "heads")
    prior_rank_t = shifted(rank_t[rank:], "ctx", 1)
    bias = jnp.where(lax.axis_index("ctx") == 0, NEGATIVE, 0.0).astype(F32).reshape(1)
    inner = inner_prior = None
    ups = []
    for index, first in enumerate(range(0, heads, per_call)):
        prior_keys, prior_values = prior[index]
        one, one_prior, upq, upk, upv = attention(
            first,
            per_call,
            bias,
            rank_t,
            prior_rank_t,
            frozen_query_rows,
            output_gradient,
            frozen_key_rows,
            prior_keys,
            frozen_value_rows,
            prior_values,
            query_up_weight,
            key_up_weight,
            value_up_weight,
        )
        inner = one if inner is None else inner + one
        inner_prior = one_prior if inner_prior is None else inner_prior + one_prior
        ups.append((upq, upk, upv))
    back = shifted(inner_prior, "ctx", -1)
    inner = jnp.concatenate([inner[:rank], inner[rank:] + back], axis=0)
    inner = summed(inner, "heads")
    high, middle, low = split3(inner)
    parts = jnp.concatenate([high, middle, low], axis=0)
    down_parts = lax.dot_general(
        parts, activations, (((1,), (1,)), ((), ())), preferred_element_type=F32
    )
    down_t = down_parts[: 3 * rank] + down_parts[3 * rank : 6 * rank] + down_parts[6 * rank :]
    pieces = [down_t[kind * rank : (kind + 1) * rank] for kind in range(3)]
    pieces += [jnp.concatenate([up[kind] for up in ups], axis=1) for kind in range(3)]
    packed = ADAPTER_SCALE * jnp.concatenate(pieces, axis=1)
    unit = 128 * lax.axis_size("ctx")
    packed = jnp.pad(packed, ((0, 0), (0, -packed.shape[1] % unit)))
    packed = reduced(packed, "ctx")
    results = []
    start = 0
    for piece in pieces:
        results.append(packed[:, start : start + piece.shape[1]])
        start += piece.shape[1]
    dq, dk, dv, upq, upk, upv = results
    return dq.T, upq, dk.T, upk, dv.T, upv


def solution(mesh):
    in_specs = (
        P("heads", "ctx"),
        P("ctx", "heads"),
        P("ctx", "heads"),
        P("ctx", "heads"),
        P("ctx", "heads"),
        P("heads", None),
        P(None, "heads"),
        P("heads", None),
        P(None, "heads"),
        P("heads", None),
        P(None, "heads"),
    )
    out_specs = (
        P("heads", None),
        P(None, "heads"),
        P("heads", None),
        P(None, "heads"),
        P("heads", None),
        P(None, "heads"),
    )
    return jax.shard_map(
        on_device, mesh=mesh, in_specs=in_specs, out_specs=out_specs, check_vma=False
    )
```

```python
import functools

import jax
import jax.numpy as jnp
from jax import lax
from jax.experimental import pallas as pl
from jax.experimental.pallas import tpu as pltpu
from jax.sharding import PartitionSpec as P

HEAD_WIDTH = 128
WINDOW = 1024
ADAPTER_SCALE = 2.0
NEGATIVE = -1e30
LOG2E = 1.4426950408889634
F32 = jnp.float32
BF16 = jnp.bfloat16


def split2(x):
    high = x.astype(BF16)
    return high, (x - high.astype(F32)).astype(BF16)


def split3(x):
    high = x.astype(BF16)
    rest = x - high.astype(F32)
    middle = rest.astype(BF16)
    return high, middle, (rest - middle.astype(F32)).astype(BF16)


def dot_nn(a, b):
    return lax.dot_general(a, b, (((1,), (0,)), ((), ())), preferred_element_type=F32)


def dot_nt(a, b):
    return lax.dot_general(a, b, (((1,), (1,)), ((), ())), preferred_element_type=F32)


def fold8(x, reduce):
    return reduce(x.reshape(x.shape[0] // 8, 8, x.shape[1]), axis=0)


def alternate(*streams):
    waiting = list(streams)
    while waiting:
        for stream in list(waiting):
            if next(stream, None) is None:
                waiting.remove(stream)


def attention_body(
    group,
    rank,
    rows,
    bias_ref,
    rank_ref,
    prior_rank_ref,
    fq_ref,
    do_ref,
    fk_ref,
    pk_ref,
    fv_ref,
    pv_ref,
    uq_ref,
    uk_ref,
    uv_ref,
    inner_ref,
    inner_prior_ref,
    upq_ref,
    upk_ref,
    upv_ref,
    ranks_t,
    ranks,
    k_all,
    v_all,
    k_t,
    dk_acc,
    dv_acc,
    s_scr,
    dp_scr,
    ds_scr,
):
    head = pl.program_id(0)
    own = fk_ref.shape[0]
    width = HEAD_WIDTH
    tiles = own // rows
    half = rows // 2
    lanes = group * rows
    scale = width**-0.5
    factor = scale * LOG2E

    @pl.when(head == 0)
    def _():
        mine = split3(rank_ref[...])
        prior = split3(prior_rank_ref[...])
        blank = jnp.zeros((rank, own), BF16)
        for part in range(3):
            at = part * 3 * rank
            ranks_t[at : at + 3 * rank, own:] = mine[part]
            ranks_t[at : at + rank, :own] = blank
            ranks_t[at + rank : at + 3 * rank, :own] = prior[part]
        ranks[...] = ranks_t[...].astype(F32).T.astype(BF16)
        inner_ref[...] = jnp.zeros_like(inner_ref)
        inner_prior_ref[...] = jnp.zeros_like(inner_prior_ref)

    def stacked(up, kind):
        pieces = []
        for _ in range(3):
            for other in range(3):
                pieces.append(up if other == kind else jnp.zeros_like(up))
        return jnp.concatenate(pieces, axis=0)

    def rank_rows(kind, start, size):
        pieces = [
            ranks_t[(3 * part + kind) * rank : (3 * part + kind + 1) * rank, start : start + size]
            for part in range(3)
        ]
        return jnp.concatenate(pieces, axis=0)

    def merged(x):
        return x[:rank] + x[rank : 2 * rank] + x[2 * rank :]

    def lifted(base, lift):
        return (base.astype(F32) + ADAPTER_SCALE * lift).astype(BF16)

    up_kv = jnp.concatenate([stacked(uk_ref[...], 1), stacked(uv_ref[...], 2)], axis=1)
    up_q = stacked(uq_ref[...], 0)
    for start in range(0, 2 * own, rows):
        lift = dot_nn(ranks[start : start + rows], up_kv)
        source_k, source_v, at = (pk_ref, pv_ref, start) if start < own else (fk_ref, fv_ref, start - own)
        keys = lifted(source_k[at : at + rows], lift[:, :width])
        k_all[start : start + rows] = keys
        k_t[:, start : start + rows] = keys.T
        v_all[start : start + rows] = lifted(source_v[at : at + rows], lift[:, width:])

    key_at = lax.broadcasted_iota(jnp.int32, (rows, lanes), 0)
    lane = lax.broadcasted_iota(jnp.int32, (rows, lanes), 1)
    earlier = key_at > lax.div(lane, group * half) * half + lax.rem(lane, half)
    bias = bias_ref[0]
    state = [{} for _ in range(tiles)]

    def across(x):
        return jnp.concatenate(
            [
                x[part * half : (part + 1) * half, g * width : (g + 1) * width].T
                for part in range(rows // half)
                for g in range(group)
            ],
            axis=1,
        )

    def tile_rows(block, tile):
        start = (block + tile) * rows
        return slice(start, start + rows)

    def tile_bias(block, tile):
        return bias if 0 < tile and block + tile < tiles else None

    def products(block):
        slot = block % 2
        here = slice(block * rows, (block + 1) * rows)
        lift = dot_nn(ranks[own + block * rows : own + (block + 1) * rows], up_q)
        q_t = across(lifted(fq_ref[here], lift))
        do_t = across(do_ref[here])
        highest = None
        for tile in range(tiles):
            scores = dot_nn(k_all[tile_rows(block, tile)], q_t)
            grads = dot_nn(v_all[tile_rows(block, tile)], do_t)
            if tile == 0:
                last = dot_nn(k_all[tile_rows(block, tiles)], q_t)
                scores = jnp.where(earlier, scores + bias, last)
                grads = jnp.where(earlier, grads, dot_nn(v_all[tile_rows(block, tiles)], do_t))
            s_scr[slot, tile] = scores
            dp_scr[slot, tile] = grads
            high = fold8(scores, jnp.max)
            if tile_bias(block, tile) is not None:
                high = high + bias
            highest = high if highest is None else jnp.maximum(highest, high)
            yield True
        state[block].update(q_t=q_t, do_t=do_t, highest=highest)

    def exponents(block):
        slot = block % 2
        top = jnp.max(state[block]["highest"], axis=0, keepdims=True) * factor
        shifted_top = top - bias
        total = dots = None
        for tile in range(tiles):
            minus = top if tile_bias(block, tile) is None else shifted_top
            exponent = jnp.exp2(s_scr[slot, tile] * factor - minus)
            s_scr[slot, tile] = exponent
            one = fold8(exponent, jnp.sum)
            two = fold8(exponent * dp_scr[slot, tile], jnp.sum)
            total = one if total is None else total + one
            dots = two if dots is None else dots + two
            yield True
        inverse = 1.0 / jnp.sum(total, axis=0, keepdims=True)
        state[block].update(
            inverse=inverse,
            row_dots=jnp.sum(dots, axis=0, keepdims=True) * inverse,
            do_scaled=(state[block]["do_t"].astype(F32) * inverse).astype(BF16),
            q_scaled=(state[block]["q_t"].astype(F32) * inverse).astype(BF16),
        )

    def accumulate(acc, block, tile, value):
        fresh = block == 0 or tile == tiles
        if fresh:
            acc[:, tile_rows(block, tile)] = value
        else:
            acc[:, tile_rows(block, tile)] += value

    def gradients(block):
        slot = block % 2
        now = state[block]
        for tile in range(tiles):
            exponent = s_scr[slot, tile]
            grad = exponent * (dp_scr[slot, tile] - now["row_dots"])
            if tile == 0:
                zero = jnp.zeros_like(grad)
                parts = [
                    (0, jnp.where(earlier, grad, zero), jnp.where(earlier, exponent, zero)),
                    (tiles, jnp.where(earlier, zero, grad), jnp.where(earlier, zero, exponent)),
                ]
            else:
                parts = [(tile, grad, exponent)]
            for to, grad, exponent in parts:
                grad_low = grad.astype(BF16)
                ds_scr[slot, to * rows : (to + 1) * rows] = grad_low
                accumulate(dk_acc, block, to, dot_nt(now["q_scaled"], grad_low))
                accumulate(dv_acc, block, to, dot_nt(now["do_scaled"], exponent.astype(BF16)))
            yield True
        window = slice(block * rows, (block + tiles + 1) * rows)
        dq = dot_nn(k_t[:, window], ds_scr[slot]) * (now["inverse"] * scale)
        dq = dq.astype(BF16)
        up = uq_ref[...]
        rank_q = rank_rows(0, own + block * rows, rows)
        for part in range(rows // half):
            at = part * group * half
            tall = jnp.concatenate(
                [dq[:, at + g * half : at + (g + 1) * half] for g in range(group)], axis=0
            )
            start = block * rows + part * half
            inner_ref[:rank, start : start + half] += dot_nn(up, tall)
        for g in range(group):
            head_dq = jnp.concatenate(
                [
                    dq[:, (part * group + g) * half : (part * group + g + 1) * half]
                    for part in range(rows // half)
                ],
                axis=1,
            )
            value = merged(dot_nt(rank_q, head_dq))
            columns = slice(g * width, (g + 1) * width)
            if block == 0:
                upq_ref[:, columns] = value
            else:
                upq_ref[:, columns] += value

    alternate(products(0))
    alternate(products(1), exponents(0))
    for block in range(tiles):
        streams = [gradients(block)]
        if block + 2 < tiles:
            streams.append(products(block + 2))
        if block + 1 < tiles:
            streams.append(exponents(block + 1))
        alternate(*streams)

    for kind, acc, up_ref, out_ref, mult in (
        (1, dk_acc, uk_ref, upk_ref, scale),
        (2, dv_acc, uv_ref, upv_ref, 1.0),
    ):
        low = (acc[...] * mult).astype(BF16)
        out_ref[...] = merged(dot_nt(rank_rows(kind, 0, 2 * own), low))
        inner = dot_nn(up_ref[...], low)
        inner_prior_ref[(kind - 1) * rank : kind * rank, :] += inner[:, :own]
        inner_ref[kind * rank : (kind + 1) * rank, :] += inner[:, own:]


def attention(first, heads, bias, rank_t, prior_rank_t, fq, do, fk, fv, packed, uq, uk, uv, rows=256):
    rank = uq.shape[0]
    own = fk.shape[0]
    width = HEAD_WIDTH
    group = fq.shape[1] // fk.shape[1]
    wide = group * width
    tiles = own // rows
    lanes = group * rows
    whole = lambda h: (0, 0)
    key = lambda h: (0, first + h)
    chunk = lambda h: (0, h)
    in_specs = [
        pl.BlockSpec(memory_space=pltpu.SMEM),
        pl.BlockSpec(rank_t.shape, whole),
        pl.BlockSpec(prior_rank_t.shape, whole),
        pl.BlockSpec((own, wide), key),
        pl.BlockSpec((own, wide), key),
        pl.BlockSpec((own, width), key),
        pl.BlockSpec((own, width), chunk),
        pl.BlockSpec((own, width), key),
        pl.BlockSpec((own, width), lambda h: (0, heads + h)),
        pl.BlockSpec((rank, wide), key),
        pl.BlockSpec((rank, width), key),
        pl.BlockSpec((rank, width), key),
    ]
    out_specs = [
        pl.BlockSpec((3 * rank, own), whole),
        pl.BlockSpec((2 * rank, own), whole),
        pl.BlockSpec((rank, wide), chunk),
        pl.BlockSpec((rank, width), chunk),
        pl.BlockSpec((rank, width), chunk),
    ]
    out_shape = [
        jax.ShapeDtypeStruct((3 * rank, own), F32),
        jax.ShapeDtypeStruct((2 * rank, own), F32),
        jax.ShapeDtypeStruct((rank, heads * wide), F32),
        jax.ShapeDtypeStruct((rank, heads * width), F32),
        jax.ShapeDtypeStruct((rank, heads * width), F32),
    ]
    scratch = [
        pltpu.VMEM((9 * rank, 2 * own), BF16),
        pltpu.VMEM((2 * own, 9 * rank), BF16),
        pltpu.VMEM((2 * own, width), BF16),
        pltpu.VMEM((2 * own, width), BF16),
        pltpu.VMEM((width, 2 * own), BF16),
        pltpu.VMEM((width, 2 * own), F32),
        pltpu.VMEM((width, 2 * own), F32),
        pltpu.VMEM((2, tiles, rows, lanes), F32),
        pltpu.VMEM((2, tiles, rows, lanes), F32),
        pltpu.VMEM((2, (tiles + 1) * rows, lanes), BF16),
    ]
    pairs = heads * group * own * own
    return pl.pallas_call(
        functools.partial(attention_body, group, rank, rows),
        grid=(heads,),
        in_specs=in_specs,
        out_specs=out_specs,
        out_shape=out_shape,
        scratch_shapes=scratch,
        compiler_params=pltpu.CompilerParams(
            dimension_semantics=("arbitrary",), vmem_limit_bytes=48 * 2**20
        ),
        cost_estimate=pl.CostEstimate(
            flops=10 * pairs * width,
            transcendentals=pairs,
            bytes_accessed=heads * own * width * (4 * group + 8),
        ),
        name="banded_attention",
    )(bias, rank_t, prior_rank_t, fq, do, fk, packed, fv, packed, uq, uk, uv)


def shifted(shard, axis, by):
    length = lax.axis_size(axis)
    pairs = [(i, i + by) for i in range(length) if 0 <= i + by < length]
    return lax.ppermute(shard, axis, pairs)


def exchanged(shard, axis, step):
    length = lax.axis_size(axis)
    return lax.ppermute(shard, axis, [(i, i ^ step) for i in range(length)])


def summed(shard, axis, kind):
    length = lax.axis_size(axis)
    if length & (length - 1):
        return lax.psum(shard, axis)
    step = 1
    while step < length:
        shard = shard + exchanged(shard.astype(kind), axis, step).astype(F32)
        step *= 2
    return shard


def reduced(shard, axis, halvings=2):
    length = lax.axis_size(axis)
    if length & (length - 1):
        return lax.psum(shard, axis)
    index = lax.axis_index(axis)
    steps = [1 << bit for bit in range(length.bit_length() - 1)]
    for step in steps[:halvings]:
        half = shard.shape[1] // 2
        first, second = shard[:, :half], shard[:, half:]
        low = (index // step) % 2 == 0
        kept = jnp.where(low, first, second)
        sent = jnp.where(low, second, first).astype(BF16)
        shard = kept + exchanged(sent, axis, step).astype(F32)
    for step in steps[halvings:]:
        sent = shard.astype(BF16)
        shard = sent.astype(F32) + exchanged(sent, axis, step).astype(F32)
    shard = shard.astype(BF16)
    for step in reversed(steps[:halvings]):
        low = (index // step) % 2 == 0
        other = exchanged(shard, axis, step)
        first, second = jnp.where(low, shard, other), jnp.where(low, other, shard)
        shard = jnp.concatenate([first, second], axis=1)
    return shard.astype(F32)


def portions(heads):
    if heads < 8:
        return [heads]
    return [heads // 4, heads // 4, heads // 2]


def on_device(
    activations,
    frozen_query_rows,
    frozen_key_rows,
    frozen_value_rows,
    output_gradient,
    query_down_weight,
    query_up_weight,
    key_down_weight,
    key_up_weight,
    value_down_weight,
    value_up_weight,
):
    rank = query_down_weight.shape[1]
    heads = frozen_key_rows.shape[1] // HEAD_WIDTH
    down = jnp.concatenate([query_down_weight, key_down_weight, value_down_weight], axis=1)
    partial_rank = lax.dot_general(
        down, activations, (((0,), (0,)), ((), ())), preferred_element_type=F32
    )
    rank_t = summed(partial_rank, "heads", F32)
    prior_rank_t = shifted(rank_t[rank:], "ctx", 1)
    prior = []
    first = 0
    for count in portions(heads):
        columns = slice(first * HEAD_WIDTH, (first + count) * HEAD_WIDTH)
        packed = jnp.concatenate(
            [frozen_key_rows[:, columns], frozen_value_rows[:, columns]], axis=1
        )
        if first:
            packed, _ = lax.optimization_barrier((packed, rank_t))
        prior.append((first, count, shifted(packed, "ctx", 1)))
        first += count
    bias = jnp.where(lax.axis_index("ctx") == 0, NEGATIVE, 0.0).astype(F32).reshape(1)
    inner = inner_prior = None
    ups = []
    for first, count, packed in prior:
        one, one_prior, upq, upk, upv = attention(
            first,
            count,
            bias,
            rank_t,
            prior_rank_t,
            frozen_query_rows,
            output_gradient,
            frozen_key_rows,
            frozen_value_rows,
            packed,
            query_up_weight,
            key_up_weight,
            value_up_weight,
        )
        inner = one if inner is None else inner + one
        inner_prior = one_prior if inner_prior is None else inner_prior + one_prior
        ups.append((upq, upk, upv))
    back = shifted(inner_prior.astype(BF16), "ctx", -1).astype(F32)
    inner = jnp.concatenate([inner[:rank], inner[rank:] + back], axis=0)
    inner = summed(inner, "heads", BF16)
    parts = jnp.concatenate(split2(inner), axis=0)
    down_parts = lax.dot_general(
        parts, activations, (((1,), (1,)), ((), ())), preferred_element_type=F32
    )
    down_t = down_parts[: 3 * rank] + down_parts[3 * rank :]
    pieces = [down_t[kind * rank : (kind + 1) * rank] for kind in range(3)]
    pieces += [jnp.concatenate([up[kind] for up in ups], axis=1) for kind in range(3)]
    packed = ADAPTER_SCALE * jnp.concatenate(pieces, axis=1)
    packed = jnp.pad(packed, ((0, 0), (0, -packed.shape[1] % 512)))
    packed = reduced(packed, "ctx")
    results = []
    start = 0
    for piece in pieces:
        results.append(packed[:, start : start + piece.shape[1]])
        start += piece.shape[1]
    dq, dk, dv, upq, upk, upv = results
    return dq.T, upq, dk.T, upk, dv.T, upv


def solution(mesh):
    in_specs = (
        P("heads", "ctx"),
        P("ctx", "heads"),
        P("ctx", "heads"),
        P("ctx", "heads"),
        P("ctx", "heads"),
        P("heads", None),
        P(None, "heads"),
        P("heads", None),
        P(None, "heads"),
        P("heads", None),
        P(None, "heads"),
    )
    out_specs = (
        P("heads", None),
        P(None, "heads"),
        P("heads", None),
        P(None, "heads"),
        P("heads", None),
        P(None, "heads"),
    )
    return jax.shard_map(
        on_device, mesh=mesh, in_specs=in_specs, out_specs=out_specs, check_vma=False
    )
```

```python
import functools

import jax
import jax.numpy as jnp
from jax import lax
from jax.experimental import pallas as pl
from jax.experimental.pallas import tpu as pltpu
from jax.sharding import PartitionSpec as P


HEAD_WIDTH = 128
ADAPTER_SCALE = 2.0
NEGATIVE = -1e30
LOG2E = 1.4426950408889634
F32 = jnp.float32
BF16 = jnp.bfloat16


def split2(x):
    high = x.astype(BF16)
    return high, (x - high.astype(F32)).astype(BF16)


def split3(x):
    high = x.astype(BF16)
    rest = x - high.astype(F32)
    middle = rest.astype(BF16)
    return high, middle, (rest - middle.astype(F32)).astype(BF16)


def dot_nn(a, b):
    return lax.dot_general(a, b, (((1,), (0,)), ((), ())), preferred_element_type=F32)


def dot_nt(a, b):
    return lax.dot_general(a, b, (((1,), (1,)), ((), ())), preferred_element_type=F32)


def fold8(x, reduce):
    return reduce(x.reshape(x.shape[0] // 8, 8, x.shape[1]), axis=0)


def alternate(*streams):
    waiting = list(streams)
    while waiting:
        for stream in list(waiting):
            if next(stream, None) is None:
                waiting.remove(stream)


def attention_body(
    group,
    rank,
    rows,
    bias_ref,
    rank_ref,
    prior_rank_ref,
    fq_ref,
    do_ref,
    fk_ref,
    pk_ref,
    fv_ref,
    pv_ref,
    uq_ref,
    uk_ref,
    uv_ref,
    inner_ref,
    inner_prior_ref,
    upq_ref,
    upk_ref,
    upv_ref,
    ranks_t,
    ranks,
    k_all,
    v_all,
    k_t,
    dk_acc,
    dv_acc,
    s_scr,
    dp_scr,
    ds_scr,
):
    head = pl.program_id(0)
    own = fk_ref.shape[0]
    width = HEAD_WIDTH
    tiles = own // rows
    half = rows // 2
    lanes = group * rows
    scale = width**-0.5
    factor = scale * LOG2E

    @pl.when(head == 0)
    def _():
        mine = split3(rank_ref[...])
        prior = split3(prior_rank_ref[...])
        blank = jnp.zeros((rank, own), BF16)
        for part in range(3):
            at = part * 3 * rank
            ranks_t[at : at + 3 * rank, own:] = mine[part]
            ranks_t[at : at + rank, :own] = blank
            ranks_t[at + rank : at + 3 * rank, :own] = prior[part]
        ranks[...] = ranks_t[...].astype(F32).T.astype(BF16)
        inner_ref[...] = jnp.zeros_like(inner_ref)
        inner_prior_ref[...] = jnp.zeros_like(inner_prior_ref)

    def stacked(up, kind):
        pieces = []
        for _ in range(3):
            for other in range(3):
                pieces.append(up if other == kind else jnp.zeros_like(up))
        return jnp.concatenate(pieces, axis=0)

    def rank_rows(kind, start, size):
        pieces = [
            ranks_t[(3 * part + kind) * rank : (3 * part + kind + 1) * rank, start : start + size]
            for part in range(3)
        ]
        return jnp.concatenate(pieces, axis=0)

    def merged(x):
        return x[:rank] + x[rank : 2 * rank] + x[2 * rank :]

    def lifted(base, lift):
        return (base.astype(F32) + ADAPTER_SCALE * lift).astype(BF16)

    up_kv = jnp.concatenate([stacked(uk_ref[...], 1), stacked(uv_ref[...], 2)], axis=1)
    up_q = stacked(uq_ref[...], 0)
    for start in range(0, 2 * own, rows):
        lift = dot_nn(ranks[start : start + rows], up_kv)
        source_k, source_v, at = (pk_ref, pv_ref, start) if start < own else (fk_ref, fv_ref, start - own)
        keys = lifted(source_k[at : at + rows], lift[:, :width])
        k_all[start : start + rows] = keys
        k_t[:, start : start + rows] = keys.T
        v_all[start : start + rows] = lifted(source_v[at : at + rows], lift[:, width:])

    key_at = lax.broadcasted_iota(jnp.int32, (rows, lanes), 0)
    lane = lax.broadcasted_iota(jnp.int32, (rows, lanes), 1)
    earlier = key_at > lax.div(lane, group * half) * half + lax.rem(lane, half)
    bias = bias_ref[0]
    state = [{} for _ in range(tiles)]

    def across(x):
        return jnp.concatenate(
            [
                x[part * half : (part + 1) * half, g * width : (g + 1) * width].T
                for part in range(rows // half)
                for g in range(group)
            ],
            axis=1,
        )

    def tile_rows(block, tile):
        start = (block + tile) * rows
        return slice(start, start + rows)

    def tile_bias(block, tile):
        return bias if 0 < tile and block + tile < tiles else None

    def products(block):
        slot = block % 2
        here = slice(block * rows, (block + 1) * rows)
        lift = dot_nn(ranks[own + block * rows : own + (block + 1) * rows], up_q)
        q_t = across(lifted(fq_ref[here], lift))
        do_t = across(do_ref[here])
        highest = None
        for tile in range(tiles):
            scores = dot_nn(k_all[tile_rows(block, tile)], q_t)
            grads = dot_nn(v_all[tile_rows(block, tile)], do_t)
            if tile == 0:
                last = dot_nn(k_all[tile_rows(block, tiles)], q_t)
                scores = jnp.where(earlier, scores + bias, last)
                grads = jnp.where(earlier, grads, dot_nn(v_all[tile_rows(block, tiles)], do_t))
            s_scr[slot, tile] = scores
            dp_scr[slot, tile] = grads
            high = fold8(scores, jnp.max)
            if tile_bias(block, tile) is not None:
                high = high + bias
            highest = high if highest is None else jnp.maximum(highest, high)
            yield True
        state[block].update(q_t=q_t, do_t=do_t, highest=highest)

    def exponents(block):
        slot = block % 2
        top = jnp.max(state[block]["highest"], axis=0, keepdims=True) * factor
        shifted_top = top - bias
        total = dots = None
        for tile in range(tiles):
            minus = top if tile_bias(block, tile) is None else shifted_top
            exponent = jnp.exp2(s_scr[slot, tile] * factor - minus)
            s_scr[slot, tile] = exponent
            one = fold8(exponent, jnp.sum)
            two = fold8(exponent * dp_scr[slot, tile], jnp.sum)
            total = one if total is None else total + one
            dots = two if dots is None else dots + two
            yield True
        inverse = 1.0 / jnp.sum(total, axis=0, keepdims=True)
        state[block].update(
            inverse=inverse,
            row_dots=jnp.sum(dots, axis=0, keepdims=True) * inverse,
            do_scaled=(state[block]["do_t"].astype(F32) * inverse).astype(BF16),
            q_scaled=(state[block]["q_t"].astype(F32) * inverse).astype(BF16),
        )

    def accumulate(acc, block, tile, value):
        fresh = block == 0 or tile == tiles
        if fresh:
            acc[:, tile_rows(block, tile)] = value
        else:
            acc[:, tile_rows(block, tile)] += value

    def gradients(block):
        slot = block % 2
        now = state[block]
        for tile in range(tiles):
            exponent = s_scr[slot, tile]
            grad = exponent * (dp_scr[slot, tile] - now["row_dots"])
            if tile == 0:
                zero = jnp.zeros_like(grad)
                parts = [
                    (0, jnp.where(earlier, grad, zero), jnp.where(earlier, exponent, zero)),
                    (tiles, jnp.where(earlier, zero, grad), jnp.where(earlier, zero, exponent)),
                ]
            else:
                parts = [(tile, grad, exponent)]
            for to, grad, exponent in parts:
                grad_low = grad.astype(BF16)
                ds_scr[slot, to * rows : (to + 1) * rows] = grad_low
                accumulate(dk_acc, block, to, dot_nt(now["q_scaled"], grad_low))
                accumulate(dv_acc, block, to, dot_nt(now["do_scaled"], exponent.astype(BF16)))
            yield True
        window = slice(block * rows, (block + tiles + 1) * rows)
        dq = dot_nn(k_t[:, window], ds_scr[slot]) * (now["inverse"] * scale)
        dq = dq.astype(BF16)
        up = uq_ref[...]
        rank_q = rank_rows(0, own + block * rows, rows)
        for part in range(rows // half):
            at = part * group * half
            tall = jnp.concatenate(
                [dq[:, at + g * half : at + (g + 1) * half] for g in range(group)], axis=0
            )
            start = block * rows + part * half
            inner_ref[:rank, start : start + half] += dot_nn(up, tall)
        for g in range(group):
            head_dq = jnp.concatenate(
                [
                    dq[:, (part * group + g) * half : (part * group + g + 1) * half]
                    for part in range(rows // half)
                ],
                axis=1,
            )
            value = merged(dot_nt(rank_q, head_dq))
            columns = slice(g * width, (g + 1) * width)
            if block == 0:
                upq_ref[:, columns] = value
            else:
                upq_ref[:, columns] += value

    alternate(products(0))
    alternate(products(1), exponents(0))
    for block in range(tiles):
        streams = [gradients(block)]
        if block + 2 < tiles:
            streams.append(products(block + 2))
        if block + 1 < tiles:
            streams.append(exponents(block + 1))
        alternate(*streams)

    for kind, acc, up_ref, out_ref, mult in (
        (1, dk_acc, uk_ref, upk_ref, scale),
        (2, dv_acc, uv_ref, upv_ref, 1.0),
    ):
        low = (acc[...] * mult).astype(BF16)
        out_ref[...] = merged(dot_nt(rank_rows(kind, 0, 2 * own), low))
        inner = dot_nn(up_ref[...], low)
        inner_prior_ref[(kind - 1) * rank : kind * rank, :] += inner[:, :own]
        inner_ref[kind * rank : (kind + 1) * rank, :] += inner[:, own:]


def attention(first, heads, bias, rank_t, prior_rank_t, fq, do, fk, fv, packed, uq, uk, uv, rows=256):
    rank = uq.shape[0]
    own = fk.shape[0]
    width = HEAD_WIDTH
    group = fq.shape[1] // fk.shape[1]
    wide = group * width
    tiles = own // rows
    lanes = group * rows
    whole = lambda h: (0, 0)
    key = lambda h: (0, first + h)
    chunk = lambda h: (0, h)
    in_specs = [
        pl.BlockSpec(memory_space=pltpu.SMEM),
        pl.BlockSpec(rank_t.shape, whole),
        pl.BlockSpec(prior_rank_t.shape, whole),
        pl.BlockSpec((own, wide), key),
        pl.BlockSpec((own, wide), key),
        pl.BlockSpec((own, width), key),
        pl.BlockSpec((own, width), chunk),
        pl.BlockSpec((own, width), key),
        pl.BlockSpec((own, width), lambda h: (0, heads + h)),
        pl.BlockSpec((rank, wide), key),
        pl.BlockSpec((rank, width), key),
        pl.BlockSpec((rank, width), key),
    ]
    out_specs = [
        pl.BlockSpec((3 * rank, own), whole),
        pl.BlockSpec((2 * rank, own), whole),
        pl.BlockSpec((rank, wide), chunk),
        pl.BlockSpec((rank, width), chunk),
        pl.BlockSpec((rank, width), chunk),
    ]
    out_shape = [
        jax.ShapeDtypeStruct((3 * rank, own), F32),
        jax.ShapeDtypeStruct((2 * rank, own), F32),
        jax.ShapeDtypeStruct((rank, heads * wide), F32),
        jax.ShapeDtypeStruct((rank, heads * width), F32),
        jax.ShapeDtypeStruct((rank, heads * width), F32),
    ]
    scratch = [
        pltpu.VMEM((9 * rank, 2 * own), BF16),
        pltpu.VMEM((2 * own, 9 * rank), BF16),
        pltpu.VMEM((2 * own, width), BF16),
        pltpu.VMEM((2 * own, width), BF16),
        pltpu.VMEM((width, 2 * own), BF16),
        pltpu.VMEM((width, 2 * own), F32),
        pltpu.VMEM((width, 2 * own), F32),
        pltpu.VMEM((2, tiles, rows, lanes), F32),
        pltpu.VMEM((2, tiles, rows, lanes), F32),
        pltpu.VMEM((2, (tiles + 1) * rows, lanes), BF16),
    ]
    pairs = heads * group * own * own
    return pl.pallas_call(
        functools.partial(attention_body, group, rank, rows),
        grid=(heads,),
        in_specs=in_specs,
        out_specs=out_specs,
        out_shape=out_shape,
        scratch_shapes=scratch,
        compiler_params=pltpu.CompilerParams(
            dimension_semantics=("arbitrary",), vmem_limit_bytes=67_000_000
        ),
        cost_estimate=pl.CostEstimate(
            flops=10 * pairs * width,
            transcendentals=pairs,
            bytes_accessed=heads * own * width * (4 * group + 8),
        ),
        name="banded_attention",
    )(bias, rank_t, prior_rank_t, fq, do, fk, packed, fv, packed, uq, uk, uv)


def shifted(shard, axis, by):
    length = lax.axis_size(axis)
    pairs = [(i, i + by) for i in range(length) if 0 <= i + by < length]
    return lax.ppermute(shard, axis, pairs)


def exchanged(shard, axis, step):
    length = lax.axis_size(axis)
    return lax.ppermute(shard, axis, [(i, i ^ step) for i in range(length)])


def summed(shard, axis, kind):
    length = lax.axis_size(axis)
    if length & (length - 1):
        return lax.psum(shard, axis)
    step = 1
    while step < length:
        shard = shard + exchanged(shard.astype(kind), axis, step).astype(F32)
        step *= 2
    return shard


def reduced(shard, axis, halvings=2):
    length = lax.axis_size(axis)
    if length & (length - 1):
        return lax.psum(shard, axis)
    index = lax.axis_index(axis)
    steps = [1 << bit for bit in range(length.bit_length() - 1)]
    for step in steps[:halvings]:
        half = shard.shape[1] // 2
        first, second = shard[:, :half], shard[:, half:]
        low = (index // step) % 2 == 0
        kept = jnp.where(low, first, second)
        sent = jnp.where(low, second, first).astype(BF16)
        shard = kept + exchanged(sent, axis, step).astype(F32)
    for step in steps[halvings:]:
        sent = shard.astype(BF16)
        shard = sent.astype(F32) + exchanged(sent, axis, step).astype(F32)
    shard = shard.astype(BF16)
    for step in reversed(steps[:halvings]):
        low = (index // step) % 2 == 0
        other = exchanged(shard, axis, step)
        first, second = jnp.where(low, shard, other), jnp.where(low, other, shard)
        shard = jnp.concatenate([first, second], axis=1)
    return shard.astype(F32)


def portions(heads):
    if heads < 8:
        return [heads]
    return [heads // 4, heads // 4, heads // 2]


def layer(
    activations,
    frozen_query_rows,
    frozen_key_rows,
    frozen_value_rows,
    output_gradient,
    query_down_weight,
    query_up_weight,
    key_down_weight,
    key_up_weight,
    value_down_weight,
    value_up_weight,
):
    rank = query_down_weight.shape[1]
    heads = frozen_key_rows.shape[1] // HEAD_WIDTH
    down = jnp.concatenate([query_down_weight, key_down_weight, value_down_weight], axis=1)
    partial_rank = lax.dot_general(
        down, activations, (((0,), (0,)), ((), ())), preferred_element_type=F32
    )
    rank_t = summed(partial_rank, "heads", F32)
    prior_rank_t = shifted(rank_t[rank:], "ctx", 1)
    prior = []
    first = 0
    for count in portions(heads):
        columns = slice(first * HEAD_WIDTH, (first + count) * HEAD_WIDTH)
        packed = jnp.concatenate(
            [frozen_key_rows[:, columns], frozen_value_rows[:, columns]], axis=1
        )
        prior.append((first, count, shifted(packed, "ctx", 1)))
        first += count
    bias = jnp.where(lax.axis_index("ctx") == 0, NEGATIVE, 0.0).astype(F32).reshape(1)
    inner = inner_prior = None
    ups = []
    for first, count, packed in prior:
        one, one_prior, upq, upk, upv = attention(
            first,
            count,
            bias,
            rank_t,
            prior_rank_t,
            frozen_query_rows,
            output_gradient,
            frozen_key_rows,
            frozen_value_rows,
            packed,
            query_up_weight,
            key_up_weight,
            value_up_weight,
        )
        inner = one if inner is None else inner + one
        inner_prior = one_prior if inner_prior is None else inner_prior + one_prior
        ups.append((upq, upk, upv))
    back = shifted(inner_prior.astype(BF16), "ctx", -1).astype(F32)
    inner = jnp.concatenate([inner[:rank], inner[rank:] + back], axis=0)
    inner = summed(inner, "heads", BF16)
    parts = jnp.concatenate(split2(inner), axis=0)
    down_parts = lax.dot_general(
        parts, activations, (((1,), (1,)), ((), ())), preferred_element_type=F32
    )
    down_t = down_parts[: 3 * rank] + down_parts[3 * rank :]
    pieces = [down_t[kind * rank : (kind + 1) * rank] for kind in range(3)]
    pieces += [jnp.concatenate([up[kind] for up in ups], axis=1) for kind in range(3)]
    packed = ADAPTER_SCALE * jnp.concatenate(pieces, axis=1)
    packed = jnp.pad(packed, ((0, 0), (0, -packed.shape[1] % 512)))
    packed = reduced(packed, "ctx")
    results = []
    start = 0
    for piece in pieces:
        results.append(packed[:, start : start + piece.shape[1]])
        start += piece.shape[1]
    dq, dk, dv, upq, upk, upv = results
    return dq.T, upq, dk.T, upk, dv.T, upv


def solution(mesh):
    in_specs = (
        P("heads", "ctx"),
        P("ctx", "heads"),
        P("ctx", "heads"),
        P("ctx", "heads"),
        P("ctx", "heads"),
        P("heads", None),
        P(None, "heads"),
        P("heads", None),
        P(None, "heads"),
        P("heads", None),
        P(None, "heads"),
    )
    out_specs = (
        P("heads", None),
        P(None, "heads"),
        P("heads", None),
        P(None, "heads"),
        P("heads", None),
        P(None, "heads"),
    )
    return jax.shard_map(layer, mesh=mesh, in_specs=in_specs, out_specs=out_specs, check_vma=False)
```

```python
import functools

import jax
import jax.numpy as jnp
from jax import lax
from jax.experimental import pallas as pl
from jax.experimental.pallas import tpu as pltpu
from jax.sharding import PartitionSpec as P


HEAD_WIDTH = 128
ADAPTER_SCALE = 2.0
NEGATIVE = -1e30
LOG2E = 1.4426950408889634
F32 = jnp.float32
BF16 = jnp.bfloat16


def split2(x):
    high = x.astype(BF16)
    return high, (x - high.astype(F32)).astype(BF16)


def split3(x):
    high = x.astype(BF16)
    rest = x - high.astype(F32)
    middle = rest.astype(BF16)
    return high, middle, (rest - middle.astype(F32)).astype(BF16)


def dot_nn(a, b):
    return lax.dot_general(a, b, (((1,), (0,)), ((), ())), preferred_element_type=F32)


def dot_nt(a, b):
    return lax.dot_general(a, b, (((1,), (1,)), ((), ())), preferred_element_type=F32)


def fold8(x, reduce):
    return reduce(x.reshape(x.shape[0] // 8, 8, x.shape[1]), axis=0)


def alternate(*streams):
    waiting = list(streams)
    while waiting:
        for stream in list(waiting):
            if next(stream, None) is None:
                waiting.remove(stream)


def attention_body(
    group,
    rank,
    rows,
    fresh,
    bias_ref,
    before_ref,
    before_prior_ref,
    rank_ref,
    prior_rank_ref,
    fq_ref,
    do_ref,
    fk_ref,
    pk_ref,
    fv_ref,
    pv_ref,
    uq_ref,
    uk_ref,
    uv_ref,
    inner_ref,
    inner_prior_ref,
    prior_low_ref,
    upq_ref,
    upk_ref,
    upv_ref,
    ranks_t,
    ranks,
    k_all,
    v_all,
    k_t,
    dk_acc,
    dv_acc,
    s_scr,
    dp_scr,
    ds_scr,
    e_scr,
):
    head = pl.program_id(0)
    own = fk_ref.shape[0]
    width = HEAD_WIDTH
    tiles = own // rows
    half = rows
    lanes = group * rows
    scale = width**-0.5
    factor = scale * LOG2E

    @pl.when(head == 0)
    def _():
        mine = split3(rank_ref[...])
        prior = split3(prior_rank_ref[...])
        blank = jnp.zeros((rank, own), BF16)
        for part in range(3):
            at = part * 3 * rank
            ranks_t[at : at + 3 * rank, own:] = mine[part]
            ranks_t[at : at + rank, :own] = blank
            ranks_t[at + rank : at + 3 * rank, :own] = prior[part]
        ranks[...] = ranks_t[...].astype(F32).T.astype(BF16)
        if fresh:
            inner_ref[...] = jnp.zeros_like(inner_ref)
            inner_prior_ref[...] = jnp.zeros_like(inner_prior_ref)
        else:
            inner_ref[...] = before_ref[...]
            inner_prior_ref[...] = before_prior_ref[...]

    def stacked(up, kind):
        pieces = []
        for _ in range(3):
            for other in range(3):
                pieces.append(up if other == kind else jnp.zeros_like(up))
        return jnp.concatenate(pieces, axis=0)

    def rank_rows(kind, start, size):
        pieces = [
            ranks_t[(3 * part + kind) * rank : (3 * part + kind + 1) * rank, start : start + size]
            for part in range(3)
        ]
        return jnp.concatenate(pieces, axis=0)

    def merged(x):
        return x[:rank] + x[rank : 2 * rank] + x[2 * rank :]

    def lifted(base, lift):
        return (base.astype(F32) + ADAPTER_SCALE * lift).astype(BF16)

    up_kv = jnp.concatenate([stacked(uk_ref[...], 1), stacked(uv_ref[...], 2)], axis=1)
    up_q = stacked(uq_ref[...], 0)
    for start in range(0, 2 * own, rows):
        lift = dot_nn(ranks[start : start + rows], up_kv)
        source_k, source_v, at = (pk_ref, pv_ref, start) if start < own else (fk_ref, fv_ref, start - own)
        keys = lifted(source_k[at : at + rows], lift[:, :width])
        k_all[start : start + rows] = keys
        k_t[:, start : start + rows] = keys.T
        v_all[start : start + rows] = lifted(source_v[at : at + rows], lift[:, width:])

    key_at = lax.broadcasted_iota(jnp.int32, (rows, lanes), 0)
    lane = lax.broadcasted_iota(jnp.int32, (rows, lanes), 1)
    earlier = key_at > lax.div(lane, group * half) * half + lax.rem(lane, half)
    bias = bias_ref[0]
    state = [{} for _ in range(tiles)]

    def across(x):
        return jnp.concatenate(
            [
                x[part * half : (part + 1) * half, g * width : (g + 1) * width].T
                for part in range(rows // half)
                for g in range(group)
            ],
            axis=1,
        )

    def tile_bias(block, tile):
        return bias if 0 < tile and block + tile < tiles else None

    def products(block):
        slot = block % 2
        here = slice(block * rows, (block + 1) * rows)
        lift = dot_nn(ranks[own + block * rows : own + (block + 1) * rows], up_q)
        q_t = across(lifted(fq_ref[here], lift))
        do_t = across(do_ref[here])
        highest = None
        window = slice(block * rows, (block + tiles + 1) * rows)
        all_scores = dot_nn(k_all[window], q_t)
        all_grads = dot_nn(v_all[window], do_t)
        for tile in range(tiles):
            scores = all_scores[tile * rows : (tile + 1) * rows]
            grads = all_grads[tile * rows : (tile + 1) * rows]
            if tile == 0:
                scores = jnp.where(earlier, scores + bias, all_scores[tiles * rows :])
                grads = jnp.where(earlier, grads, all_grads[tiles * rows :])
            s_scr[slot, tile] = scores
            dp_scr[slot, tile] = grads
            high = fold8(scores, jnp.max)
            if tile_bias(block, tile) is not None:
                high = high + bias
            highest = high if highest is None else jnp.maximum(highest, high)
            yield True
        state[block].update(q_t=q_t, do_t=do_t, highest=highest)

    def exponents(block):
        slot = block % 2
        top = jnp.max(state[block]["highest"], axis=0, keepdims=True) * factor
        shifted_top = top - bias
        total = dots = None
        for tile in range(tiles):
            minus = top if tile_bias(block, tile) is None else shifted_top
            exponent = jnp.exp2(s_scr[slot, tile] * factor - minus)
            s_scr[slot, tile] = exponent
            one = fold8(exponent, jnp.sum)
            two = fold8(exponent * dp_scr[slot, tile], jnp.sum)
            total = one if total is None else total + one
            dots = two if dots is None else dots + two
            yield True
        inverse = 1.0 / jnp.sum(total, axis=0, keepdims=True)
        state[block].update(
            inverse=inverse,
            row_dots=jnp.sum(dots, axis=0, keepdims=True) * inverse,
            do_scaled=(state[block]["do_t"].astype(F32) * inverse).astype(BF16),
            q_scaled=(state[block]["q_t"].astype(F32) * inverse).astype(BF16),
        )

    def gradients(block):
        slot = block % 2
        now = state[block]
        for tile in range(tiles):
            exponent = s_scr[slot, tile]
            grad = exponent * (dp_scr[slot, tile] - now["row_dots"])
            if tile == 0:
                zero = jnp.zeros_like(grad)
                parts = [
                    (0, jnp.where(earlier, grad, zero), jnp.where(earlier, exponent, zero)),
                    (tiles, jnp.where(earlier, zero, grad), jnp.where(earlier, zero, exponent)),
                ]
            else:
                parts = [(tile, grad, exponent)]
            for to, grad, exponent in parts:
                grad_low = grad.astype(BF16)
                ds_scr[slot, to * rows : (to + 1) * rows] = grad_low
                e_scr[slot, to * rows : (to + 1) * rows] = exponent.astype(BF16)
            yield True
        window = slice(block * rows, (block + tiles + 1) * rows)
        for acc, left, right in ((dk_acc, now["q_scaled"], ds_scr), (dv_acc, now["do_scaled"], e_scr)):
            value = dot_nt(left, right[slot])
            if block:
                edge = (block + tiles) * rows
                acc[:, block * rows : edge] += value[:, : tiles * rows]
                acc[:, edge : edge + rows] = value[:, tiles * rows :]
            else:
                acc[:, window] = value
        dq = dot_nn(k_t[:, window], ds_scr[slot]) * (now["inverse"] * scale)
        dq = dq.astype(BF16)
        up = uq_ref[...]
        rank_q = rank_rows(0, own + block * rows, rows)
        for part in range(rows // half):
            at = part * group * half
            tall = jnp.concatenate(
                [dq[:, at + g * half : at + (g + 1) * half] for g in range(group)], axis=0
            )
            start = block * rows + part * half
            inner_ref[:rank, start : start + half] += dot_nn(up, tall)
        for g in range(group):
            head_dq = jnp.concatenate(
                [
                    dq[:, (part * group + g) * half : (part * group + g + 1) * half]
                    for part in range(rows // half)
                ],
                axis=1,
            )
            value = merged(dot_nt(rank_q, head_dq))
            columns = slice(g * width, (g + 1) * width)
            if block == 0:
                upq_ref[:, columns] = value
            else:
                upq_ref[:, columns] += value

    alternate(products(0))
    for block in range(tiles):
        alternate(exponents(block))
        if block + 1 < tiles:
            alternate(products(block + 1))
        alternate(gradients(block))

    for kind, acc, up_ref, out_ref, mult in (
        (1, dk_acc, uk_ref, upk_ref, scale),
        (2, dv_acc, uv_ref, upv_ref, 1.0),
    ):
        low = (acc[...] * mult).astype(BF16)
        out_ref[...] = merged(dot_nt(rank_rows(kind, 0, 2 * own), low))
        inner = dot_nn(up_ref[...], low)
        inner_prior_ref[(kind - 1) * rank : kind * rank, :] += inner[:, :own]
        inner_ref[kind * rank : (kind + 1) * rank, :] += inner[:, own:]
    prior_low_ref[...] = inner_prior_ref[...].astype(BF16)


def attention(first, heads, bias, before, before_prior, rank_t, prior_rank_t, fq, do, fk, fv, packed, uq, uk, uv, rows=256):
    rank = uq.shape[0]
    own = fk.shape[0]
    width = HEAD_WIDTH
    group = fq.shape[1] // fk.shape[1]
    wide = group * width
    tiles = own // rows
    lanes = group * rows
    whole = lambda h: (0, 0)
    key = lambda h: (0, first + h)
    chunk = lambda h: (0, h)
    in_specs = [
        pl.BlockSpec(memory_space=pltpu.SMEM),
        pl.BlockSpec(before.shape, whole),
        pl.BlockSpec(before_prior.shape, whole),
        pl.BlockSpec(rank_t.shape, whole),
        pl.BlockSpec(prior_rank_t.shape, whole),
        pl.BlockSpec((own, wide), key),
        pl.BlockSpec((own, wide), key),
        pl.BlockSpec((own, width), key),
        pl.BlockSpec((own, width), chunk),
        pl.BlockSpec((own, width), key),
        pl.BlockSpec((own, width), lambda h: (0, heads + h)),
        pl.BlockSpec((rank, wide), key),
        pl.BlockSpec((rank, width), key),
        pl.BlockSpec((rank, width), key),
    ]
    out_specs = [
        pl.BlockSpec((3 * rank, own), whole),
        pl.BlockSpec((2 * rank, own), whole),
        pl.BlockSpec((2 * rank, own), whole),
        pl.BlockSpec((rank, wide), chunk),
        pl.BlockSpec((rank, width), chunk),
        pl.BlockSpec((rank, width), chunk),
    ]
    out_shape = [
        jax.ShapeDtypeStruct((3 * rank, own), F32),
        jax.ShapeDtypeStruct((2 * rank, own), F32),
        jax.ShapeDtypeStruct((2 * rank, own), BF16),
        jax.ShapeDtypeStruct((rank, heads * wide), F32),
        jax.ShapeDtypeStruct((rank, heads * width), F32),
        jax.ShapeDtypeStruct((rank, heads * width), F32),
    ]
    scratch = [
        pltpu.VMEM((9 * rank, 2 * own), BF16),
        pltpu.VMEM((2 * own, 9 * rank), BF16),
        pltpu.VMEM((2 * own, width), BF16),
        pltpu.VMEM((2 * own, width), BF16),
        pltpu.VMEM((width, 2 * own), BF16),
        pltpu.VMEM((width, 2 * own), F32),
        pltpu.VMEM((width, 2 * own), F32),
        pltpu.VMEM((2, tiles, rows, lanes), F32),
        pltpu.VMEM((2, tiles, rows, lanes), F32),
        pltpu.VMEM((2, (tiles + 1) * rows, lanes), BF16),
        pltpu.VMEM((2, (tiles + 1) * rows, lanes), BF16),
    ]
    pairs = heads * group * own * own
    return pl.pallas_call(
        functools.partial(attention_body, group, rank, rows, first == 0),
        grid=(heads,),
        in_specs=in_specs,
        out_specs=out_specs,
        out_shape=out_shape,
        scratch_shapes=scratch,
        compiler_params=pltpu.CompilerParams(
            dimension_semantics=("arbitrary",), vmem_limit_bytes=67_000_000
        ),
        cost_estimate=pl.CostEstimate(
            flops=10 * pairs * width,
            transcendentals=pairs,
            bytes_accessed=heads * own * width * (4 * group + 8),
        ),
        name="banded_attention",
    )(bias, before, before_prior, rank_t, prior_rank_t, fq, do, fk, packed, fv, packed, uq, uk, uv)


def shifted(shard, axis, by):
    length = lax.axis_size(axis)
    pairs = [(i, i + by) for i in range(length) if 0 <= i + by < length]
    return lax.ppermute(shard, axis, pairs)


def exchanged(shard, axis, step):
    length = lax.axis_size(axis)
    return lax.ppermute(shard, axis, [(i, i ^ step) for i in range(length)])


def summed(shard, axis, kind):
    length = lax.axis_size(axis)
    if length & (length - 1):
        return lax.psum(shard, axis)
    step = 1
    while step < length:
        shard = shard + exchanged(shard.astype(kind), axis, step).astype(F32)
        step *= 2
    return shard


def reduced(shard, axis, halvings=2):
    length = lax.axis_size(axis)
    if length & (length - 1):
        return lax.psum(shard, axis)
    index = lax.axis_index(axis)
    steps = [1 << bit for bit in range(length.bit_length() - 1)]
    for step in steps[:halvings]:
        half = shard.shape[1] // 2
        first, second = shard[:, :half], shard[:, half:]
        low = (index // step) % 2 == 0
        kept = jnp.where(low, first, second)
        sent = jnp.where(low, second, first).astype(BF16)
        shard = kept + exchanged(sent, axis, step).astype(F32)
    for step in steps[halvings:]:
        sent = shard.astype(BF16)
        shard = sent.astype(F32) + exchanged(sent, axis, step).astype(F32)
    shard = shard.astype(BF16)
    for step in reversed(steps[:halvings]):
        low = (index // step) % 2 == 0
        other = exchanged(shard, axis, step)
        first, second = jnp.where(low, shard, other), jnp.where(low, other, shard)
        shard = jnp.concatenate([first, second], axis=1)
    return shard.astype(F32)


def portions(heads):
    if heads < 8:
        return [heads]
    return [heads // 4, heads // 4, heads // 2]


def layer(
    activations,
    frozen_query_rows,
    frozen_key_rows,
    frozen_value_rows,
    output_gradient,
    query_down_weight,
    query_up_weight,
    key_down_weight,
    key_up_weight,
    value_down_weight,
    value_up_weight,
):
    rank = query_down_weight.shape[1]
    heads = frozen_key_rows.shape[1] // HEAD_WIDTH
    down = jnp.concatenate([query_down_weight, key_down_weight, value_down_weight], axis=1)
    partial_rank = lax.dot_general(
        down, activations, (((0,), (0,)), ((), ())), preferred_element_type=F32
    )
    rank_t = summed(partial_rank, "heads", F32)
    prior_rank_t = shifted(rank_t[rank:], "ctx", 1)
    prior = []
    first = 0
    for count in portions(heads):
        columns = slice(first * HEAD_WIDTH, (first + count) * HEAD_WIDTH)
        packed = jnp.concatenate(
            [frozen_key_rows[:, columns], frozen_value_rows[:, columns]], axis=1
        )
        prior.append((first, count, shifted(packed, "ctx", 1)))
        first += count
    bias = jnp.where(lax.axis_index("ctx") == 0, NEGATIVE, 0.0).astype(F32).reshape(1)
    inner, inner_prior = rank_t, prior_rank_t
    ups = []
    for first, count, packed in prior:
        inner, inner_prior, prior_low, upq, upk, upv = attention(
            first,
            count,
            bias,
            inner,
            inner_prior,
            rank_t,
            prior_rank_t,
            frozen_query_rows,
            output_gradient,
            frozen_key_rows,
            frozen_value_rows,
            packed,
            query_up_weight,
            key_up_weight,
            value_up_weight,
        )
        ups.append((upq, upk, upv))
    back = shifted(prior_low, "ctx", -1).astype(F32)
    inner = inner + jnp.pad(back, ((rank, 0), (0, 0)))
    inner = summed(inner, "heads", BF16)
    parts = jnp.concatenate(split2(inner), axis=0)
    down_parts = lax.dot_general(
        parts, activations, (((1,), (1,)), ((), ())), preferred_element_type=F32
    )
    down_t = down_parts[: 3 * rank] + down_parts[3 * rank :]
    pieces = [down_t[kind * rank : (kind + 1) * rank] for kind in range(3)]
    pieces += [jnp.concatenate([up[kind] for up in ups], axis=1) for kind in range(3)]
    packed = ADAPTER_SCALE * jnp.concatenate(pieces, axis=1)
    packed = jnp.pad(packed, ((0, 0), (0, -packed.shape[1] % 512)))
    packed = reduced(packed, "ctx")
    results = []
    start = 0
    for piece in pieces:
        results.append(packed[:, start : start + piece.shape[1]])
        start += piece.shape[1]
    dq, dk, dv, upq, upk, upv = results
    return dq.T, upq, dk.T, upk, dv.T, upv


def solution(mesh):
    in_specs = (
        P("heads", "ctx"),
        P("ctx", "heads"),
        P("ctx", "heads"),
        P("ctx", "heads"),
        P("ctx", "heads"),
        P("heads", None),
        P(None, "heads"),
        P("heads", None),
        P(None, "heads"),
        P("heads", None),
        P(None, "heads"),
    )
    out_specs = (
        P("heads", None),
        P(None, "heads"),
        P("heads", None),
        P(None, "heads"),
        P("heads", None),
        P(None, "heads"),
    )
    return jax.shard_map(layer, mesh=mesh, in_specs=in_specs, out_specs=out_specs, check_vma=False)
```

```python
import functools

import jax
import jax.numpy as jnp
from jax import lax
from jax.experimental import pallas as pl
from jax.experimental.pallas import tpu as pltpu
from jax.sharding import PartitionSpec as P


HEAD_WIDTH = 128
ADAPTER_SCALE = 2.0
NEGATIVE = -1e30
LOG2E = 1.4426950408889634
F32 = jnp.float32
BF16 = jnp.bfloat16


def split3(x):
    high = x.astype(BF16)
    rest = x - high.astype(F32)
    middle = rest.astype(BF16)
    return high, middle, (rest - middle.astype(F32)).astype(BF16)


def dot_nn(a, b):
    return lax.dot_general(a, b, (((1,), (0,)), ((), ())), preferred_element_type=F32)


def dot_nt(a, b):
    return lax.dot_general(a, b, (((1,), (1,)), ((), ())), preferred_element_type=F32)


def fold8(x, reduce):
    return reduce(x.reshape(x.shape[0] // 8, 8, x.shape[1]), axis=0)


def alternate(*streams):
    waiting = list(streams)
    while waiting:
        for stream in list(waiting):
            if next(stream, None) is None:
                waiting.remove(stream)


def attention_body(
    group,
    rank,
    rows,
    fresh,
    bias_ref,
    before_ref,
    before_prior_ref,
    rank_ref,
    prior_rank_ref,
    fq_ref,
    do_ref,
    fk_ref,
    pk_ref,
    fv_ref,
    pv_ref,
    uq_ref,
    uk_ref,
    uv_ref,
    inner_ref,
    inner_prior_ref,
    prior_low_ref,
    upq_ref,
    upk_ref,
    upv_ref,
    ranks_t,
    ranks,
    k_all,
    v_all,
    k_t,
    dk_acc,
    dv_acc,
    s_scr,
    dp_scr,
    ds_scr,
    e_scr,
):
    head = pl.program_id(0)
    own = fk_ref.shape[0]
    width = HEAD_WIDTH
    tiles = own // rows
    half = rows
    lanes = group * rows
    scale = width**-0.5
    factor = scale * LOG2E

    @pl.when(head == 0)
    def _():
        mine = split3(rank_ref[...])
        prior = split3(prior_rank_ref[...])
        blank = jnp.zeros((rank, own), BF16)
        for part in range(3):
            at = part * 3 * rank
            ranks_t[at : at + 3 * rank, own:] = mine[part]
            ranks_t[at : at + rank, :own] = blank
            ranks_t[at + rank : at + 3 * rank, :own] = prior[part]
        ranks[...] = ranks_t[...].astype(F32).T.astype(BF16)
        if fresh:
            inner_ref[...] = jnp.zeros_like(inner_ref)
            inner_prior_ref[...] = jnp.zeros_like(inner_prior_ref)
        else:
            inner_ref[...] = before_ref[...]
            inner_prior_ref[...] = before_prior_ref[...]

    def stacked(up, kind):
        pieces = []
        for _ in range(3):
            for other in range(3):
                pieces.append(up if other == kind else jnp.zeros_like(up))
        return jnp.concatenate(pieces, axis=0)

    def rank_rows(kind, start, size):
        pieces = [
            ranks_t[(3 * part + kind) * rank : (3 * part + kind + 1) * rank, start : start + size]
            for part in range(3)
        ]
        return jnp.concatenate(pieces, axis=0)

    def merged(x):
        return x[:rank] + x[rank : 2 * rank] + x[2 * rank :]

    def lifted(base, lift):
        return (base.astype(F32) + ADAPTER_SCALE * lift).astype(BF16)

    up_kv = jnp.concatenate([stacked(uk_ref[...], 1), stacked(uv_ref[...], 2)], axis=1)
    up_q = stacked(uq_ref[...], 0)
    for start in range(0, 2 * own, rows):
        lift = dot_nn(ranks[start : start + rows], up_kv)
        source_k, source_v, at = (pk_ref, pv_ref, start) if start < own else (fk_ref, fv_ref, start - own)
        keys = lifted(source_k[at : at + rows], lift[:, :width])
        k_all[start : start + rows] = keys
        k_t[:, start : start + rows] = keys.T
        v_all[start : start + rows] = lifted(source_v[at : at + rows], lift[:, width:])

    key_at = lax.broadcasted_iota(jnp.int32, (rows, lanes), 0)
    lane = lax.broadcasted_iota(jnp.int32, (rows, lanes), 1)
    earlier = key_at > lax.div(lane, group * half) * half + lax.rem(lane, half)
    bias = bias_ref[0]
    state = [{} for _ in range(tiles)]

    def across(x):
        return jnp.concatenate(
            [
                x[part * half : (part + 1) * half, g * width : (g + 1) * width].T
                for part in range(rows // half)
                for g in range(group)
            ],
            axis=1,
        )

    def tile_bias(block, tile):
        return bias if 0 < tile and block + tile < tiles else None

    def products(block):
        slot = block % 2
        here = slice(block * rows, (block + 1) * rows)
        lift = dot_nn(ranks[own + block * rows : own + (block + 1) * rows], up_q)
        q_t = across(lifted(fq_ref[here], lift))
        do_t = across(do_ref[here])
        highest = None
        window = slice(block * rows, (block + tiles + 1) * rows)
        all_scores = dot_nn(k_all[window], q_t)
        all_grads = dot_nn(v_all[window], do_t)
        for tile in range(tiles):
            scores = all_scores[tile * rows : (tile + 1) * rows]
            grads = all_grads[tile * rows : (tile + 1) * rows]
            if tile == 0:
                scores = jnp.where(earlier, scores + bias, all_scores[tiles * rows :])
                grads = jnp.where(earlier, grads, all_grads[tiles * rows :])
            s_scr[slot, tile] = scores
            dp_scr[slot, tile] = grads
            high = fold8(scores, jnp.max)
            if tile_bias(block, tile) is not None:
                high = high + bias
            highest = high if highest is None else jnp.maximum(highest, high)
            yield True
        state[block].update(q_t=q_t, do_t=do_t, highest=highest)

    def exponents(block):
        slot = block % 2
        top = jnp.max(state[block]["highest"], axis=0, keepdims=True) * factor
        shifted_top = top - bias
        total = dots = None
        for tile in range(tiles):
            minus = top if tile_bias(block, tile) is None else shifted_top
            exponent = jnp.exp2(s_scr[slot, tile] * factor - minus)
            s_scr[slot, tile] = exponent
            one = fold8(exponent, jnp.sum)
            two = fold8(exponent * dp_scr[slot, tile], jnp.sum)
            total = one if total is None else total + one
            dots = two if dots is None else dots + two
            yield True
        inverse = 1.0 / jnp.sum(total, axis=0, keepdims=True)
        state[block].update(
            inverse=inverse,
            row_dots=jnp.sum(dots, axis=0, keepdims=True) * inverse,
            do_scaled=(state[block]["do_t"].astype(F32) * inverse).astype(BF16),
            q_scaled=(state[block]["q_t"].astype(F32) * inverse).astype(BF16),
        )

    def gradients(block):
        slot = block % 2
        now = state[block]
        for tile in range(tiles):
            exponent = s_scr[slot, tile]
            grad = exponent * (dp_scr[slot, tile] - now["row_dots"])
            if tile == 0:
                zero = jnp.zeros_like(grad)
                parts = [
                    (0, jnp.where(earlier, grad, zero), jnp.where(earlier, exponent, zero)),
                    (tiles, jnp.where(earlier, zero, grad), jnp.where(earlier, zero, exponent)),
                ]
            else:
                parts = [(tile, grad, exponent)]
            for to, grad, exponent in parts:
                grad_low = grad.astype(BF16)
                ds_scr[slot, to * rows : (to + 1) * rows] = grad_low
                e_scr[slot, to * rows : (to + 1) * rows] = exponent.astype(BF16)
            yield True
        window = slice(block * rows, (block + tiles + 1) * rows)
        for acc, left, right in ((dk_acc, now["q_scaled"], ds_scr), (dv_acc, now["do_scaled"], e_scr)):
            value = dot_nt(left, right[slot])
            if block:
                edge = (block + tiles) * rows
                acc[:, block * rows : edge] += value[:, : tiles * rows]
                acc[:, edge : edge + rows] = value[:, tiles * rows :]
            else:
                acc[:, window] = value
        dq = dot_nn(k_t[:, window], ds_scr[slot]) * (now["inverse"] * scale)
        dq = dq.astype(BF16)
        up = uq_ref[...]
        rank_q = rank_rows(0, own + block * rows, rows)
        for part in range(rows // half):
            at = part * group * half
            tall = jnp.concatenate(
                [dq[:, at + g * half : at + (g + 1) * half] for g in range(group)], axis=0
            )
            start = block * rows + part * half
            inner_ref[:rank, start : start + half] += dot_nn(up, tall)
        for g in range(group):
            head_dq = jnp.concatenate(
                [
                    dq[:, (part * group + g) * half : (part * group + g + 1) * half]
                    for part in range(rows // half)
                ],
                axis=1,
            )
            value = merged(dot_nt(rank_q, head_dq))
            columns = slice(g * width, (g + 1) * width)
            if block == 0:
                upq_ref[:, columns] = value
            else:
                upq_ref[:, columns] += value

    alternate(products(0))
    for block in range(tiles):
        alternate(exponents(block))
        if block + 1 < tiles:
            alternate(products(block + 1))
        alternate(gradients(block))

    for kind, acc, up_ref, out_ref, mult in (
        (1, dk_acc, uk_ref, upk_ref, scale),
        (2, dv_acc, uv_ref, upv_ref, 1.0),
    ):
        low = (acc[...] * mult).astype(BF16)
        out_ref[...] = merged(dot_nt(rank_rows(kind, 0, 2 * own), low))
        inner = dot_nn(up_ref[...], low)
        inner_prior_ref[(kind - 1) * rank : kind * rank, :] += inner[:, :own]
        inner_ref[kind * rank : (kind + 1) * rank, :] += inner[:, own:]
    prior_low_ref[...] = inner_prior_ref[...].astype(BF16)


def attention(first, heads, bias, before, before_prior, rank_t, prior_rank_t, fq, do, fk, fv, packed, uq, uk, uv, rows=256):
    rank = uq.shape[0]
    own = fk.shape[0]
    width = HEAD_WIDTH
    group = fq.shape[1] // fk.shape[1]
    wide = group * width
    tiles = own // rows
    lanes = group * rows
    whole = lambda h: (0, 0)
    key = lambda h: (0, first + h)
    chunk = lambda h: (0, h)
    in_specs = [
        pl.BlockSpec(memory_space=pltpu.SMEM),
        pl.BlockSpec(before.shape, whole),
        pl.BlockSpec(before_prior.shape, whole),
        pl.BlockSpec(rank_t.shape, whole),
        pl.BlockSpec(prior_rank_t.shape, whole),
        pl.BlockSpec((own, wide), key),
        pl.BlockSpec((own, wide), key),
        pl.BlockSpec((own, width), key),
        pl.BlockSpec((own, width), chunk),
        pl.BlockSpec((own, width), key),
        pl.BlockSpec((own, width), lambda h: (0, heads + h)),
        pl.BlockSpec((rank, wide), key),
        pl.BlockSpec((rank, width), key),
        pl.BlockSpec((rank, width), key),
    ]
    out_specs = [
        pl.BlockSpec((3 * rank, own), whole),
        pl.BlockSpec((2 * rank, own), whole),
        pl.BlockSpec((2 * rank, own), whole),
        pl.BlockSpec((rank, wide), chunk),
        pl.BlockSpec((rank, width), chunk),
        pl.BlockSpec((rank, width), chunk),
    ]
    out_shape = [
        jax.ShapeDtypeStruct((3 * rank, own), F32),
        jax.ShapeDtypeStruct((2 * rank, own), F32),
        jax.ShapeDtypeStruct((2 * rank, own), BF16),
        jax.ShapeDtypeStruct((rank, heads * wide), F32),
        jax.ShapeDtypeStruct((rank, heads * width), F32),
        jax.ShapeDtypeStruct((rank, heads * width), F32),
    ]
    scratch = [
        pltpu.VMEM((9 * rank, 2 * own), BF16),
        pltpu.VMEM((2 * own, 9 * rank), BF16),
        pltpu.VMEM((2 * own, width), BF16),
        pltpu.VMEM((2 * own, width), BF16),
        pltpu.VMEM((width, 2 * own), BF16),
        pltpu.VMEM((width, 2 * own), F32),
        pltpu.VMEM((width, 2 * own), F32),
        pltpu.VMEM((2, tiles, rows, lanes), F32),
        pltpu.VMEM((2, tiles, rows, lanes), F32),
        pltpu.VMEM((2, (tiles + 1) * rows, lanes), BF16),
        pltpu.VMEM((2, (tiles + 1) * rows, lanes), BF16),
    ]
    pairs = heads * group * own * own
    return pl.pallas_call(
        functools.partial(attention_body, group, rank, rows, first == 0),
        grid=(heads,),
        in_specs=in_specs,
        out_specs=out_specs,
        out_shape=out_shape,
        scratch_shapes=scratch,
        compiler_params=pltpu.CompilerParams(
            dimension_semantics=("arbitrary",), vmem_limit_bytes=67_000_000
        ),
        cost_estimate=pl.CostEstimate(
            flops=10 * pairs * width,
            transcendentals=pairs,
            bytes_accessed=heads * own * width * (4 * group + 8),
        ),
        name="banded_attention",
    )(bias, before, before_prior, rank_t, prior_rank_t, fq, do, fk, packed, fv, packed, uq, uk, uv)


def shifted(shard, axis, by):
    length = lax.axis_size(axis)
    pairs = [(i, i + by) for i in range(length) if 0 <= i + by < length]
    return lax.ppermute(shard, axis, pairs)


def exchanged(shard, axis, step):
    length = lax.axis_size(axis)
    return lax.ppermute(shard, axis, [(i, i ^ step) for i in range(length)])


def summed(shard, axis, kind):
    length = lax.axis_size(axis)
    if length & (length - 1):
        return lax.psum(shard, axis)
    step = 1
    while step < length:
        shard = shard + exchanged(shard.astype(kind), axis, step).astype(F32)
        step *= 2
    return shard


def reduced(shard, axis, halvings=2):
    length = lax.axis_size(axis)
    if length & (length - 1):
        return lax.psum(shard, axis)
    index = lax.axis_index(axis)
    steps = [1 << bit for bit in range(length.bit_length() - 1)]
    for step in steps[:halvings]:
        half = shard.shape[1] // 2
        first, second = shard[:, :half], shard[:, half:]
        low = (index // step) % 2 == 0
        kept = jnp.where(low, first, second)
        sent = jnp.where(low, second, first).astype(BF16)
        shard = kept + exchanged(sent, axis, step).astype(F32)
    for step in steps[halvings:]:
        sent = shard.astype(BF16)
        shard = sent.astype(F32) + exchanged(sent, axis, step).astype(F32)
    shard = shard.astype(BF16)
    for step in reversed(steps[:halvings]):
        low = (index // step) % 2 == 0
        other = exchanged(shard, axis, step)
        first, second = jnp.where(low, shard, other), jnp.where(low, other, shard)
        shard = jnp.concatenate([first, second], axis=1)
    return shard.astype(F32)


def portions(heads):
    if heads < 8:
        return [heads]
    return [heads // 4, heads // 4, heads // 2]


def layer(
    activations,
    frozen_query_rows,
    frozen_key_rows,
    frozen_value_rows,
    output_gradient,
    query_down_weight,
    query_up_weight,
    key_down_weight,
    key_up_weight,
    value_down_weight,
    value_up_weight,
):
    rank = query_down_weight.shape[1]
    heads = frozen_key_rows.shape[1] // HEAD_WIDTH
    down = jnp.concatenate([query_down_weight, key_down_weight, value_down_weight], axis=1)
    partial_rank = lax.dot_general(
        down, activations, (((0,), (0,)), ((), ())), preferred_element_type=F32
    )
    rank_t = summed(partial_rank, "heads", F32)
    prior_rank_t = shifted(rank_t[rank:], "ctx", 1)
    prior = []
    first = 0
    for count in portions(heads):
        columns = slice(first * HEAD_WIDTH, (first + count) * HEAD_WIDTH)
        packed = jnp.concatenate(
            [frozen_key_rows[:, columns], frozen_value_rows[:, columns]], axis=1
        )
        prior.append((first, count, shifted(packed, "ctx", 1)))
        first += count
    bias = jnp.where(lax.axis_index("ctx") == 0, NEGATIVE, 0.0).astype(F32).reshape(1)
    inner, inner_prior = rank_t, prior_rank_t
    ups = []
    for first, count, packed in prior:
        inner, inner_prior, prior_low, upq, upk, upv = attention(
            first,
            count,
            bias,
            inner,
            inner_prior,
            rank_t,
            prior_rank_t,
            frozen_query_rows,
            output_gradient,
            frozen_key_rows,
            frozen_value_rows,
            packed,
            query_up_weight,
            key_up_weight,
            value_up_weight,
        )
        ups.append((upq, upk, upv))
    back = shifted(prior_low, "ctx", -1).astype(F32)
    inner = inner + jnp.pad(back, ((rank, 0), (0, 0)))
    inner = summed(inner, "heads", BF16)
    down_t = lax.dot_general(
        activations, inner.astype(BF16), (((1,), (1,)), ((), ())), preferred_element_type=F32
    ).T
    pieces = [down_t[kind * rank : (kind + 1) * rank] for kind in range(3)]
    pieces += [jnp.concatenate([up[kind] for up in ups], axis=1) for kind in range(3)]
    packed = ADAPTER_SCALE * jnp.concatenate(pieces, axis=1)
    packed = jnp.pad(packed, ((0, 0), (0, -packed.shape[1] % 512)))
    packed = reduced(packed, "ctx")
    results = []
    start = 0
    for piece in pieces:
        results.append(packed[:, start : start + piece.shape[1]])
        start += piece.shape[1]
    dq, dk, dv, upq, upk, upv = results
    return dq.T, upq, dk.T, upk, dv.T, upv


def solution(mesh):
    in_specs = (
        P("heads", "ctx"),
        P("ctx", "heads"),
        P("ctx", "heads"),
        P("ctx", "heads"),
        P("ctx", "heads"),
        P("heads", None),
        P(None, "heads"),
        P("heads", None),
        P(None, "heads"),
        P("heads", None),
        P(None, "heads"),
    )
    out_specs = (
        P("heads", None),
        P(None, "heads"),
        P("heads", None),
        P(None, "heads"),
        P("heads", None),
        P(None, "heads"),
    )
    return jax.shard_map(layer, mesh=mesh, in_specs=in_specs, out_specs=out_specs, check_vma=False)
```
